128 devices in a mesh: probe: 4 (over x), tx: 8 (over z, core), ty: 4 (over y).
Axes of the slice: x: 4, y: 4, z: 4, core: 2. Of those that a mesh axis runs over, the one named last changes fastest.
Arguments:
- probes: float32 [16, 256, 128, 128], P('probe', 'tx', 'ty'), may hold values from -8 to 8
- coupling: float32 [7, 256, 128, 128], P(None, 'tx', 'ty'), may hold values from 0.05 to 0.35, as said below
- sensor_cell: int32 [4096], replicated, may hold values from 0 to 4194302, as said below
- sensor_frac: float32 [4096], replicated, may hold values from 0 to 1
- noise_var: float32 [4096], replicated, may hold values from 0.25 to 1
- owner_slot: int32 [4096], replicated, may hold values from 0 to 4095, each once
Outputs:
- gradient: float32 [4096], P(('probe', 'tx', 'ty'))
The draws below stay inside these ranges and needn't reach their ends.
Inputs may be any that keep to these rules, and one draw needn't show every extreme that they name: `sensor_cell`: each entry is the flat index (x * 128 + y) * 128 + z of a grid cell with z below 127; sensors are spread unevenly over the grid. `owner_slot`: a permutation of 0 to 4095. coupling[0] lies in 0.15 to 0.35, coupling[1] and coupling[2] in 0.16 to 0.34, the others in 0.05 to 0.115.
All inputs are finite; a program needn't handle non-finite values.
Results may differ from the reference program's by a relative error of at most 0.00023.
Values sent between devices are 32-bit elements; how exact they have to be, the bound alone decides.
A program may use at most 64 MiB of HBM per device.

```python
import math
import jax
import jax.numpy as jnp
from jax import lax

NZ = 128
STEPS = 16
SENSORS = 4096
NPROBE = 16
NX = 256
NY = 128


def draw_probes(key, part):
    normal = jax.random.normal(key, (NPROBE, NX, NY, NZ), jnp.float32)
    return jnp.clip(2.0 * normal, -8.0, 8.0)


def draw_coupling(key, part):
    uniform = jax.random.uniform(key, (7, NX, NY, NZ), jnp.float32)
    lowest = jnp.array([0.15, 0.16, 0.16, 0.05, 0.05, 0.05, 0.05], jnp.float32)
    highest = jnp.array([0.35, 0.34, 0.34, 0.115, 0.115, 0.115, 0.115], jnp.float32)
    return lowest[:, None, None, None] + (highest - lowest)[:, None, None, None] * uniform


def draw_sensor_cell(key, part):
    key_x = jax.random.fold_in(key, 11)
    key_y = jax.random.fold_in(key, 12)
    key_w = jax.random.fold_in(key, 13)
    key_z = jax.random.fold_in(key, 14)
    index_x = jax.random.randint(key_x, (SENSORS,), 0, NX)
    index_y = jnp.minimum(jax.random.randint(key_y, (SENSORS,), 0, NY), jax.random.randint(key_w, (SENSORS,), 0, NY))
    index_z = jax.random.randint(key_z, (SENSORS,), 0, NZ - 1)
    index_x = index_x.at[0].set(0).at[1].set(NX - 1)
    index_y = index_y.at[0].set(0).at[1].set(NY - 1)
    index_z = index_z.at[0].set(0).at[1].set(NZ - 2)
    return ((index_x * NY + index_y) * NZ + index_z).astype(jnp.int32)


def setup_inputs(seed: int = 0) -> dict:
    seeds = jax.random.split(jax.random.key(seed), 7)
    return {
        "probes": draw_probes(jax.random.fold_in(seeds[6], 71), 0),
        "coupling": draw_coupling(jax.random.fold_in(seeds[6], 71), 0),
        "sensor_cell": draw_sensor_cell(jax.random.fold_in(seeds[6], 71), 0),
        "sensor_frac": jnp.clip(jax.random.uniform(seeds[3], (SENSORS,), jnp.float32, 0.0, 1.0), 0.0, 1.0),
        "noise_var": jnp.clip(jnp.exp(jax.random.uniform(seeds[4], (SENSORS,), jnp.float32, math.log(0.25), math.log(1.0))), 0.25, 1.0),
        "owner_slot": jax.random.permutation(seeds[5], SENSORS).astype(jnp.int32),
    }


def advance(tracer, coupling):
    padded = jnp.pad(tracer, 1)
    result = coupling[0] * tracer
    result = result + coupling[1] * padded[2:, 1:-1, 1:-1] + coupling[2] * padded[:-2, 1:-1, 1:-1]
    result = result + coupling[3] * padded[1:-1, 2:, 1:-1] + coupling[4] * padded[1:-1, :-2, 1:-1]
    result = result + coupling[5] * padded[1:-1, 1:-1, 2:] + coupling[6] * padded[1:-1, 1:-1, :-2]
    return result


def reference(probes, coupling, sensor_cell, sensor_frac, noise_var, owner_slot):
    def adjoint(tracer):
        for number in range(STEPS):
            tracer = advance(tracer, coupling)
        flattened = tracer.reshape(-1)
        values = (1.0 - sensor_frac) * flattened[sensor_cell] + sensor_frac * flattened[sensor_cell + 1]
        return values * values

    squares = lax.map(adjoint, probes)
    weight_grad = -jnp.sum(squares, axis=0) / noise_var
    return jnp.zeros_like(weight_grad).at[owner_slot].set(weight_grad)
```

```python
import functools

import jax
import jax.numpy as jnp
from jax import lax
from jax.experimental import pallas as pl
from jax.experimental.pallas import tpu as pltpu
from jax.sharding import PartitionSpec as P

STEPS = 16
MESH = pl.DeviceIdType.MESH
GROUP = 2
LEAD = 8


def stencil_kernel(
    np_, nx, ny, probes_hbm, coup_hbm, out_hbm, va, vb, c, ysend, yrecv, load_sem, coup_sem, send_sem, recv_sem
):
    bufs = (va, vb)
    planes = nx + 2
    tx, ty = lax.axis_index("tx"), lax.axis_index("ty")
    ntx, nty = lax.axis_size("tx"), lax.axis_size("ty")
    has = (tx > 0, tx < ntx - 1, ty > 0, ty < nty - 1)
    where = ({"tx": tx - 1}, {"tx": tx + 1}, {"ty": ty - 1}, {"ty": ty + 1})

    loads = []
    for p in range(np_):
        cp = pltpu.make_async_copy(
            probes_hbm.at[p], va.at[pl.ds(p * planes + 1, nx), pl.ds(LEAD, ny)], load_sem.at[p]
        )
        cp.start()
        loads.append(cp)
    cload = []
    for k in range(7):
        cp = pltpu.make_async_copy(coup_hbm.at[k], c.at[k], coup_sem.at[k])
        cp.start()
        cload.append(cp)

    zrow = jnp.zeros((8, 128), jnp.float32)
    for buf in bufs:
        for p in range(np_):
            for q in (p * planes, p * planes + nx + 1):
                for t in range(ny // 8):
                    buf[q, pl.ds(LEAD + 8 * t, 8)] = zrow

            def zero_rows(i, _, buf=buf, p=p):
                buf[p * planes + 1 + i, pl.ds(0, 8)] = zrow
                buf[p * planes + 1 + i, pl.ds(LEAD + ny, 8)] = zrow
                return 0

            lax.fori_loop(0, nx, zero_rows, 0)

    barrier = pltpu.get_barrier_semaphore()
    for d in range(4):

        @pl.when(has[d])
        def _(d=d):
            pl.semaphore_signal(barrier, inc=1, device_id=where[d], device_id_type=MESH)

    pl.semaphore_wait(barrier, sum(h.astype(jnp.int32) for h in has))

    def copy(d, par, p):
        v = bufs[par]
        if d < 2:
            src = v.at[p * planes + (1 if d == 0 else nx), pl.ds(LEAD, ny)]
            dst = v.at[p * planes + (nx + 1 if d == 0 else 0), pl.ds(LEAD, ny)]
        else:
            src = ysend.at[par, d - 2, p]
            dst = yrecv.at[par, d - 2, p]
        return pltpu.make_async_remote_copy(
            src_ref=src,
            dst_ref=dst,
            send_sem=send_sem.at[par, d, p],
            recv_sem=recv_sem.at[par, d, p],
            device_id=where[d],
            device_id_type=MESH,
        )

    opposite = (1, 0, 3, 2)

    def pack(par, p):
        v = bufs[par]
        ysend[par, 0, p] = v[pl.ds(p * planes + 1, nx), LEAD, :]
        ysend[par, 1, p] = v[pl.ds(p * planes + 1, nx), LEAD + ny - 1, :]

    def send(par, p):
        for d in (2, 3, 0, 1):

            @pl.when(has[d])
            def _(d=d):
                copy(d, par, p).start()

    def wait_send(par, p):
        for d in range(4):

            @pl.when(has[d])
            def _(d=d):
                copy(d, par, p).wait_send()

    def receive(par, p):
        v = bufs[par]
        for d in range(4):

            @pl.when(has[opposite[d]])
            def _(d=d):
                copy(d, par, p).wait_recv()
                if d == 2:
                    v[pl.ds(p * planes + 1, nx), LEAD + ny, :] = yrecv[par, 0, p]
                if d == 3:
                    v[pl.ds(p * planes + 1, nx), LEAD - 1, :] = yrecv[par, 1, p]

    for p in range(np_):
        loads[p].wait()
        pack(0, p)
        send(0, p)
    for k in range(7):
        cload[k].wait()
    lane = lax.broadcasted_iota(jnp.int32, (8, 128), 1)

    def clip_edges(i, _):
        for t in range(ny // 8):
            rows = pl.ds(8 * t, 8)
            c[5, i, rows] = jnp.where(lane == 127, 0.0, c[5, i, rows])
            c[6, i, rows] = jnp.where(lane == 0, 0.0, c[6, i, rows])
        return 0

    lax.fori_loop(0, nx, clip_edges, 0)

    def compute(group, par):
        src, dst = bufs[par], bufs[1 - par]
        tiles = ny // 8

        def at(p, plane, t, off=0):
            return src[p * planes + plane, pl.ds(LEAD + 8 * t + off, 8)]

        def body(i, carry):
            prev, cur = carry
            nxt = []
            for t in range(tiles):
                coef = [c[k, i, pl.ds(8 * t, 8)] for k in range(7)]
                for g, p in enumerate(group):
                    n = t * len(group) + g
                    v = cur[n]
                    ahead = at(p, i + 2, t)
                    up = at(p, i + 1, t, 1)
                    down = at(p, i + 1, t, -1)
                    r = coef[0] * v
                    r = r + (coef[1] * ahead + coef[2] * prev[n])
                    r = r + (coef[3] * up + coef[4] * down)
                    r = r + (coef[5] * pltpu.roll(v, 127, 1) + coef[6] * pltpu.roll(v, 1, 1))
                    dst[p * planes + i + 1, pl.ds(LEAD + 8 * t, 8)] = r
                    nxt.append(ahead)
            return cur, tuple(nxt)

        order = [(t, p) for t in range(tiles) for p in group]
        prev = tuple(at(p, 0, t) for t, p in order)
        cur = tuple(at(p, 1, t) for t, p in order)
        lax.fori_loop(0, nx, body, (prev, cur))

    groups = [tuple(range(g, g + GROUP)) for g in range(0, np_, GROUP)]

    def two_steps(it, _):
        for par in range(2):
            for group in groups:
                for p in group:
                    receive(par, p)
                if par == 1:
                    for p in group:
                        wait_send(1 - par, p)
                else:

                    @pl.when(it > 0)
                    def _():
                        for p in group:
                            wait_send(1 - par, p)

                compute(group, par)
                if par == 0:
                    for p in group:
                        pack(1 - par, p)
                        send(1 - par, p)
                else:

                    @pl.when(it < STEPS // 2 - 1)
                    def _():
                        for p in group:
                            pack(1 - par, p)
                            send(1 - par, p)

        return 0

    lax.fori_loop(0, STEPS // 2, two_steps, 0)
    for p in range(np_):
        wait_send(1, p)
        cp = pltpu.make_async_copy(
            va.at[pl.ds(p * planes + 1, nx), pl.ds(LEAD, ny)],
            out_hbm.at[:, :, pl.ds(p * 128, 128)],
            load_sem.at[p],
        )
        cp.start()
    for p in range(np_):
        pltpu.make_async_copy(
            va.at[pl.ds(p * planes + 1, nx), pl.ds(LEAD, ny)],
            out_hbm.at[:, :, pl.ds(p * 128, 128)],
            load_sem.at[p],
        ).wait()


def stencil(probes, coupling):
    np_, nx, ny, nz = probes.shape
    planes = nx + 2
    field = pltpu.VMEM((np_ * planes, ny + 16, nz), jnp.float32)
    face = pltpu.VMEM((2, 2, np_, nx, nz), jnp.float32)
    return pl.pallas_call(
        functools.partial(stencil_kernel, np_, nx, ny),
        out_shape=jax.ShapeDtypeStruct((nx, ny, np_ * nz), jnp.float32),
        in_specs=[pl.BlockSpec(memory_space=pl.ANY)] * 2,
        out_specs=pl.BlockSpec(memory_space=pl.ANY),
        scratch_shapes=[
            field,
            field,
            pltpu.VMEM(coupling.shape, jnp.float32),
            face,
            face,
            pltpu.SemaphoreType.DMA((np_,)),
            pltpu.SemaphoreType.DMA((7,)),
            pltpu.SemaphoreType.DMA((2, 4, np_)),
            pltpu.SemaphoreType.DMA((2, 4, np_)),
        ],
        compiler_params=pltpu.CompilerParams(collective_id=0, has_side_effects=True, vmem_limit_bytes=32 << 20),
        name="stencil",
    )(probes, coupling)


def shards(probes, coupling, sensor_cell, sensor_frac, noise_var, owner_slot):
    cells_x = probes.shape[1]
    cells_y = probes.shape[2]
    depth_cells = probes.shape[3]
    tile_x = lax.axis_index("tx")
    tile_y = lax.axis_index("ty")
    total_y = cells_y * lax.axis_size("ty")
    tracer = stencil(probes, coupling)
    plane_cells = total_y * depth_cells
    global_x = sensor_cell // plane_cells
    global_y = sensor_cell // depth_cells % total_y
    global_z = sensor_cell % depth_cells
    local_x = global_x - tile_x * cells_x
    local_y = global_y - tile_y * cells_y
    inside = (local_x >= 0) & (local_x < cells_x) & (local_y >= 0) & (local_y < cells_y)
    line_index = jnp.clip(local_x, 0, cells_x - 1) * cells_y + jnp.clip(local_y, 0, cells_y - 1)
    lines = tracer.reshape(cells_x * cells_y, 4, depth_cells)
    picked = jnp.take(lines, line_index, axis=0)
    heights = jnp.arange(depth_cells, dtype=jnp.int32)[None, :]
    below_pick = (heights == global_z[:, None]).astype(jnp.float32)
    above_pick = (heights == global_z[:, None] + 1).astype(jnp.float32)
    below_value = jnp.sum(picked * below_pick[:, None], axis=2)
    above_value = jnp.sum(picked * above_pick[:, None], axis=2)
    values = (1.0 - sensor_frac)[:, None] * below_value + sensor_frac[:, None] * above_value
    energy = jnp.sum(values * values, axis=1)
    contrib = jnp.where(inside, -energy / noise_var, 0.0)
    ordered = jnp.zeros_like(contrib).at[owner_slot].set(contrib)
    return lax.psum_scatter(ordered, ("probe", "tx", "ty"), scatter_dimension=0, tiled=True)


def solution(mesh):
    in_specs = (P("probe", "tx", "ty", None), P(None, "tx", "ty", None), P(), P(), P(), P())
    out_specs = P(("probe", "tx", "ty"))
    return jax.shard_map(shards, mesh=mesh, in_specs=in_specs, out_specs=out_specs, check_vma=False)
```

```python
import functools

import jax
import jax.numpy as jnp
from jax import lax
from jax.experimental import pallas as pl
from jax.experimental.pallas import tpu as pltpu
from jax.sharding import PartitionSpec as P

STEPS = 16
MESH = pl.DeviceIdType.MESH
GROUP = 2
LEAD = 8
UNROLL = 4
CHUNK = 320


def stencil_kernel(
    np_, nx, ny, probes_hbm, coup_hbm, out_hbm, va, vb, c, ysend, yrecv, load_sem, coup_sem, send_sem, recv_sem
):
    planes = nx + 2
    rows = ny + 2 * LEAD
    bufs = (va, vb)
    flat = tuple(v.reshape(np_ * planes * rows, 128) for v in bufs)
    tx, ty = lax.axis_index("tx"), lax.axis_index("ty")
    ntx, nty = lax.axis_size("tx"), lax.axis_size("ty")
    has = (tx > 0, tx < ntx - 1, ty > 0, ty < nty - 1)
    where = ({"tx": tx - 1}, {"tx": tx + 1}, {"ty": ty - 1}, {"ty": ty + 1})

    loads = []
    for p in range(np_):
        cp = pltpu.make_async_copy(
            probes_hbm.at[p], va.at[pl.ds(p * planes + 1, nx), pl.ds(LEAD, ny)], load_sem.at[p]
        )
        cp.start()
        loads.append(cp)
    cload = []
    for k in range(7):
        cp = pltpu.make_async_copy(coup_hbm.at[k], c.at[k], coup_sem.at[k])
        cp.start()
        cload.append(cp)

    zrow = jnp.zeros((8, 128), jnp.float32)
    for buf in bufs:
        for p in range(np_):
            for q in (p * planes, p * planes + nx + 1):
                for t in range(ny // 8):
                    buf[q, pl.ds(LEAD + 8 * t, 8)] = zrow

            def zero_rows(i, _, buf=buf, p=p):
                buf[p * planes + 1 + i, pl.ds(0, 8)] = zrow
                buf[p * planes + 1 + i, pl.ds(LEAD + ny, 8)] = zrow
                return 0

            lax.fori_loop(0, nx, zero_rows, 0)

    barrier = pltpu.get_barrier_semaphore()
    for d in range(4):

        @pl.when(has[d])
        def _(d=d):
            pl.semaphore_signal(barrier, inc=1, device_id=where[d], device_id_type=MESH)

    pl.semaphore_wait(barrier, sum(h.astype(jnp.int32) for h in has))

    def copy(d, par, p):
        v = bufs[par]
        if d < 2:
            src = v.at[p * planes + (1 if d == 0 else nx), pl.ds(LEAD, ny)]
            dst = v.at[p * planes + (nx + 1 if d == 0 else 0), pl.ds(LEAD, ny)]
        else:
            src = ysend.at[par, d - 2, p]
            dst = yrecv.at[par, d - 2, p]
        return pltpu.make_async_remote_copy(
            src_ref=src,
            dst_ref=dst,
            send_sem=send_sem.at[par, d, p],
            recv_sem=recv_sem.at[par, d, p],
            device_id=where[d],
            device_id_type=MESH,
        )

    opposite = (1, 0, 3, 2)

    def face(par, p, row):
        return flat[par], pl.ds((p * planes + 1) * rows + row, nx, stride=rows)

    def pack(par, p):
        for side, row in enumerate((LEAD, LEAD + ny - 1)):
            ref, lines = face(par, p, row)
            ysend[par, side, p] = ref[lines, :]

    def send(par, p):
        for d in (2, 3, 0, 1):

            @pl.when(has[d])
            def _(d=d):
                copy(d, par, p).start()

    def wait_send(par, p):
        for d in range(4):

            @pl.when(has[d])
            def _(d=d):
                copy(d, par, p).wait_send()

    def receive(par, p):
        for d in range(4):

            @pl.when(has[opposite[d]])
            def _(d=d):
                copy(d, par, p).wait_recv()
                if d >= 2:
                    ref, at = face(par, p, LEAD + ny if d == 2 else LEAD - 1)
                    ref[at, :] = yrecv[par, d - 2, p]

    for p in range(np_):
        loads[p].wait()
        pack(0, p)
        send(0, p)
    for k in range(7):
        cload[k].wait()
    lane = lax.broadcasted_iota(jnp.int32, (8, 128), 1)

    def clip_edges(i, _):
        for t in range(ny // 8):
            rows = pl.ds(8 * t, 8)
            c[5, i, rows] = jnp.where(lane == 127, 0.0, c[5, i, rows])
            c[6, i, rows] = jnp.where(lane == 0, 0.0, c[6, i, rows])
        return 0

    lax.fori_loop(0, nx, clip_edges, 0)

    def compute(group, par):
        src, dst = bufs[par], bufs[1 - par]
        tiles = ny // 8

        def at(p, plane, t, off=0):
            return src[p * planes + plane, pl.ds(LEAD + 8 * t + off, 8)]

        def one(i, prev, cur):
            nxt = []
            for t in range(tiles):
                coef = [c[k, i, pl.ds(8 * t, 8)] for k in range(7)]
                for g, p in enumerate(group):
                    n = t * len(group) + g
                    v = cur[n]
                    ahead = at(p, i + 2, t)
                    up = at(p, i + 1, t, 1)
                    down = at(p, i + 1, t, -1)
                    r = coef[0] * v
                    r = r + (coef[1] * ahead + coef[2] * prev[n])
                    r = r + (coef[3] * up + coef[4] * down)
                    r = r + (coef[5] * pltpu.roll(v, 127, 1) + coef[6] * pltpu.roll(v, 1, 1))
                    dst[p * planes + i + 1, pl.ds(LEAD + 8 * t, 8)] = r
                    nxt.append(ahead)
            return cur, tuple(nxt)

        def body(block, carry):
            for u in range(UNROLL):
                carry = one(block * UNROLL + u, *carry)
            return carry

        order = [(t, p) for t in range(tiles) for p in group]
        prev = tuple(at(p, 0, t) for t, p in order)
        cur = tuple(at(p, 1, t) for t, p in order)
        lax.fori_loop(0, nx // UNROLL, body, (prev, cur))

    groups = [tuple(range(g, g + GROUP)) for g in range(0, np_, GROUP)]

    def two_steps(it, _):
        for par in range(2):
            for group in groups:
                for p in group:
                    receive(par, p)
                if par == 1:
                    for p in group:
                        wait_send(1 - par, p)
                else:

                    @pl.when(it > 0)
                    def _():
                        for p in group:
                            wait_send(1 - par, p)

                compute(group, par)
                if par == 0:
                    for p in group:
                        pack(1 - par, p)
                        send(1 - par, p)
                else:

                    @pl.when(it < STEPS // 2 - 1)
                    def _():
                        for p in group:
                            pack(1 - par, p)
                            send(1 - par, p)

        return 0

    lax.fori_loop(0, STEPS // 2, two_steps, 0)
    for p in range(np_):
        wait_send(1, p)
        cp = pltpu.make_async_copy(
            va.at[pl.ds(p * planes + 1, nx), pl.ds(LEAD, ny)],
            out_hbm.at[:, :, pl.ds(p * 128, 128)],
            load_sem.at[p],
        )
        cp.start()
    for p in range(np_):
        pltpu.make_async_copy(
            va.at[pl.ds(p * planes + 1, nx), pl.ds(LEAD, ny)],
            out_hbm.at[:, :, pl.ds(p * 128, 128)],
            load_sem.at[p],
        ).wait()


def stencil(probes, coupling):
    np_, nx, ny, nz = probes.shape
    planes = nx + 2
    field = pltpu.VMEM((np_ * planes, ny + 2 * LEAD, nz), jnp.float32)
    face = pltpu.VMEM((2, 2, np_, nx, nz), jnp.float32)
    return pl.pallas_call(
        functools.partial(stencil_kernel, np_, nx, ny),
        out_shape=jax.ShapeDtypeStruct((nx, ny, np_ * nz), jnp.float32),
        in_specs=[pl.BlockSpec(memory_space=pl.ANY)] * 2,
        out_specs=pl.BlockSpec(memory_space=pl.ANY),
        scratch_shapes=[
            field,
            field,
            pltpu.VMEM(coupling.shape, jnp.float32),
            face,
            face,
            pltpu.SemaphoreType.DMA((np_,)),
            pltpu.SemaphoreType.DMA((7,)),
            pltpu.SemaphoreType.DMA((2, 4, np_)),
            pltpu.SemaphoreType.DMA((2, 4, np_)),
        ],
        compiler_params=pltpu.CompilerParams(collective_id=0, has_side_effects=True, vmem_limit_bytes=32 << 20),
        name="stencil",
    )(probes, coupling)


def sense_kernel(np_, nx, ny, total_y, field, cell, frac, noise, slot, out, data):
    tx, ty = lax.axis_index("tx"), lax.axis_index("ty")
    lines, lanes = cell.shape
    bf16, f32 = jnp.bfloat16, jnp.float32

    def dot(a, b, dims=((1,), (0,))):
        return lax.dot_general(a, b, (dims, ((), ())), preferred_element_type=f32)

    def split(x):
        high = x.astype(bf16)
        rest = x - high.astype(f32)
        middle = rest.astype(bf16)
        return high, middle, (rest - middle.astype(f32)).astype(bf16)

    shift_z = 128 .bit_length() - 1
    shift_x = shift_z + total_y.bit_length() - 1
    place = cell[...]
    local_x = lax.shift_right_logical(place, shift_x) - tx * nx
    local_y = (lax.shift_right_logical(place, shift_z) & (total_y - 1)) - ty * ny
    inside = (local_x >= 0) & (local_x < nx) & (local_y >= 0) & (local_y < ny)
    ones = jnp.where(inside, 1.0, 0.0)
    count = jnp.sum(ones).astype(jnp.int32)

    def iota(shape, dim):
        return lax.broadcasted_iota(jnp.int32, shape, dim)

    upto = jnp.where(iota((lanes, lanes), 0) <= iota((lanes, lanes), 1), 1.0, 0.0).astype(bf16)
    before = jnp.where(iota((lines, lines), 1) < iota((lines, lines), 0), 1.0, 0.0).astype(bf16)
    marks = ones.astype(bf16)
    within = dot(marks, upto)
    totals = dot(marks, jnp.ones((lanes, lanes), bf16))
    rank = dot(before, totals.astype(bf16)) + within - 1.0
    rank = jnp.where(inside, rank, -1.0).astype(jnp.int32)

    def as_float(x):
        return jnp.where(inside, x, 0).astype(f32)

    parts = [as_float(local_x), as_float(local_y), as_float(place & 127)]
    parts += [lax.shift_right_logical(slot[...], shift_z).astype(f32), (slot[...] & 127).astype(f32)]
    parts += [x.astype(f32) for x in split(frac[...])] + [x.astype(f32) for x in split(noise[...])]
    for k, part in enumerate(parts):
        data[pl.ds(k, lines, stride=16), :] = part
    for k in range(len(parts), 16):
        data[pl.ds(k, lines, stride=16), :] = jnp.zeros((lines, lanes), f32)

    out[...] = jnp.zeros_like(out)
    row_id = iota((CHUNK, lanes), 0)
    lane_id = iota((CHUNK, lanes), 1)

    def chunk(n, _):
        first = n * CHUNK
        picked = jnp.zeros((CHUNK, 16), f32)
        for r in range(lines):
            hot = jnp.where(rank[r : r + 1, :] - first == row_id, 1.0, 0.0).astype(bf16)
            picked = picked + dot(hot, data[pl.ds(16 * r, 16), :].astype(bf16), ((1,), (1,)))

        def column(k):
            return picked[:, k : k + 1]

        line = (column(0) * ny + column(1)).astype(jnp.int32)
        height = column(2).astype(jnp.int32)
        high = column(3).astype(jnp.int32)
        low = column(4).astype(jnp.int32)
        part_up = column(5) + column(6) + column(7)
        variance = column(8) + column(9) + column(10)
        got = jnp.zeros((CHUNK, np_ * 128), f32)
        wide = 128
        for b in range(nx * ny // wide):
            hot = jnp.where(line - b * wide == lane_id, 1.0, 0.0).astype(bf16)
            for piece in split(field[pl.ds(b * wide, wide), :]):
                got = got + dot(hot, piece)
        weight = jnp.where(lane_id == height, 1.0 - part_up, 0.0) + jnp.where(lane_id == height + 1, part_up, 0.0)
        energy = jnp.zeros((CHUNK, 1), f32)
        for p in range(np_):
            value = jnp.sum(got[:, p * 128 : (p + 1) * 128] * weight, axis=1, keepdims=True)
            energy = energy + value * value
        valid = row_id[:, :1] + first < count
        grad = jnp.where(valid, -energy / jnp.where(valid, variance, 1.0), 0.0)
        to_line = jnp.where(iota((CHUNK, lines), 1) == high, 1.0, 0.0)
        to_lane = jnp.where(lane_id == low, grad, 0.0)
        out[...] += lax.dot_general(
            to_line, to_lane, (((0,), (0,)), ((), ())), precision=lax.Precision.HIGHEST, preferred_element_type=f32
        )
        return 0

    lax.fori_loop(0, (count + CHUNK - 1) // CHUNK, chunk, 0)


def sense(field, cell, frac, noise, slot, np_, nx, ny, total_y):
    return pl.pallas_call(
        functools.partial(sense_kernel, np_, nx, ny, total_y),
        out_shape=jax.ShapeDtypeStruct(cell.shape, jnp.float32),
        in_specs=[pl.BlockSpec(memory_space=pltpu.VMEM)] * 5,
        out_specs=pl.BlockSpec(memory_space=pltpu.VMEM),
        scratch_shapes=[pltpu.VMEM((16 * cell.shape[0], cell.shape[1]), jnp.float32)],
        compiler_params=pltpu.CompilerParams(vmem_limit_bytes=32 << 20),
        name="sense",
    )(field, cell, frac, noise, slot)


def collect_kernel(terms, out, first, rows, second, send1, recv1, send2, recv2):
    me, tx, ty = lax.axis_index("probe"), lax.axis_index("tx"), lax.axis_index("ty")
    n, ntx, nty = lax.axis_size("probe"), lax.axis_size("tx"), lax.axis_size("ty")
    probes = [{"probe": lax.rem(me + k, n)} for k in range(n)]
    pairs = [(a, b) for a in range(ntx) for b in range(nty)][1:]

    def tile(a, b):
        return {"tx": lax.rem(tx + a, ntx), "ty": lax.rem(ty + b, nty)}

    barrier = pltpu.get_barrier_semaphore()
    for k in range(1, n):
        pl.semaphore_signal(barrier, inc=1, device_id=probes[k], device_id_type=MESH)
    for a, b in pairs:
        pl.semaphore_signal(barrier, inc=1, device_id=tile(a, b), device_id_type=MESH)
    pl.semaphore_wait(barrier, n - 1 + len(pairs))

    copies = []
    for k in range(1, n):
        cp = pltpu.make_async_remote_copy(
            src_ref=terms.at[pl.ds(pl.multiple_of(lax.rem(me + k, n) * ntx, 8), ntx)],
            dst_ref=first.at[k],
            send_sem=send1.at[k],
            recv_sem=recv1.at[k],
            device_id=probes[k],
            device_id_type=MESH,
        )
        cp.start()
        copies.append(cp)
    total = terms[pl.ds(pl.multiple_of(me * ntx, 8), ntx), :]
    for k in range(1, n):
        copies[k - 1].wait_recv()
        total = total + first[k]
    for a in range(ntx):
        rows[a] = total[a : a + 1, :]
    for a, b in pairs:
        cp = pltpu.make_async_remote_copy(
            src_ref=rows.at[lax.rem(tx + a, ntx)],
            dst_ref=second.at[a * nty + b],
            send_sem=send2.at[a * nty + b],
            recv_sem=recv2.at[a * nty + b],
            device_id=tile(a, b),
            device_id_type=MESH,
        )
        cp.start()
        copies.append(cp)
    mine = rows[tx]
    for cp, (a, b) in zip(copies[n - 1 :], pairs):
        cp.wait_recv()
        mine = mine + second[a * nty + b]
    width = 128 // nty
    result = mine
    for b in range(1, nty):
        result = jnp.where(ty == b, pltpu.roll(mine, 128 - width * b, 1), result)
    out[...] = result[:, :width]
    for cp in copies:
        cp.wait_send()


def collect(terms):
    n, ntx, nty = lax.axis_size("probe"), lax.axis_size("tx"), lax.axis_size("ty")
    return pl.pallas_call(
        collect_kernel,
        out_shape=jax.ShapeDtypeStruct((1, 128 // nty), jnp.float32),
        in_specs=[pl.BlockSpec(memory_space=pltpu.VMEM)],
        out_specs=pl.BlockSpec(memory_space=pltpu.VMEM),
        scratch_shapes=[
            pltpu.VMEM((n, ntx, 128), jnp.float32),
            pltpu.VMEM((ntx, 1, 128), jnp.float32),
            pltpu.VMEM((ntx * nty, 1, 128), jnp.float32),
            pltpu.SemaphoreType.DMA((n,)),
            pltpu.SemaphoreType.DMA((n,)),
            pltpu.SemaphoreType.DMA((ntx * nty,)),
            pltpu.SemaphoreType.DMA((ntx * nty,)),
        ],
        compiler_params=pltpu.CompilerParams(collective_id=1, has_side_effects=True),
        name="collect",
    )(terms)


def shards(probes, coupling, sensor_cell, sensor_frac, noise_var, owner_slot):
    np_, nx, ny, nz = probes.shape
    field = stencil(probes, coupling).reshape(nx * ny, np_ * nz)
    small = [a.reshape(-1, 128) for a in (sensor_cell, sensor_frac, noise_var, owner_slot)]
    terms = sense(field, *small, np_, nx, ny, ny * lax.axis_size("ty"))
    return collect(terms).reshape(-1)


def solution(mesh):
    in_specs = (P("probe", "tx", "ty", None), P(None, "tx", "ty", None), P(), P(), P(), P())
    out_specs = P(("probe", "tx", "ty"))
    return jax.shard_map(shards, mesh=mesh, in_specs=in_specs, out_specs=out_specs, check_vma=False)
```

```python
import functools

import jax
import jax.numpy as jnp
from jax import lax
from jax.experimental import pallas as pl
from jax.experimental.pallas import tpu as pltpu
from jax.sharding import PartitionSpec as P

STEPS = 16
MESH = pl.DeviceIdType.MESH
LEAD = 8
UNROLL_A = 17
UNROLL_B = 16
CHUNK = 320


DIRECTIONS = ((-1, 0), (1, 0), (0, -1), (0, 1), (-1, -1), (-1, 1), (1, -1), (1, 1))
X_DIRS, Y_DIRS, CORNERS = (0, 1), (2, 3), (4, 5, 6, 7)


def stencil_kernel(
    np_, nx, ny, probes_hbm, coup_hbm, out_hbm,
    va, vb, c, cyrecv, cysend, xrecv, yrecv, krecv, ysend, ksend,
    load_sem, coup_sem, send_sem, recv_sem, csend_sem, crecv_sem,
):
    planes = nx + 4
    rows = ny + 2 * LEAD
    blocks = STEPS // 2
    fa, fb = (v.reshape(np_ * planes * rows, 128) for v in (va, vb))
    fc = c.reshape(7 * (nx + 2) * ny, 128)
    tx, ty = lax.axis_index("tx"), lax.axis_index("ty")
    ntx, nty = lax.axis_size("tx"), lax.axis_size("ty")

    def exists(sx, sy):
        return (tx + sx >= 0) & (tx + sx < ntx) & (ty + sy >= 0) & (ty + sy < nty)

    to = [exists(sx, sy) for sx, sy in DIRECTIONS]
    from_ = [exists(-sx, -sy) for sx, sy in DIRECTIONS]
    where = [{"tx": tx + sx, "ty": ty + sy} for sx, sy in DIRECTIONS]

    def load(p):
        return pltpu.make_async_copy(
            probes_hbm.at[p], va.at[pl.ds(p * planes + 2, nx), pl.ds(LEAD, ny)], load_sem.at[p]
        )

    def load_coupling(k):
        return pltpu.make_async_copy(coup_hbm.at[k], c.at[k, pl.ds(1, nx)], coup_sem.at[k])

    load(0).start()
    for k in range(7):
        load_coupling(k).start()
    for p in range(1, np_):
        load(p).start()

    tile = jnp.zeros((8, 128), jnp.float32)

    def zero_field(q, _):
        va[q, pl.ds(0, 8)] = tile
        va[q, pl.ds(LEAD + ny, 8)] = tile
        return 0

    lax.fori_loop(0, np_ * planes, zero_field, 0)
    for p in range(np_):
        for q in (0, 1, nx + 2, nx + 3):
            for t in range(ny // 8):
                va[p * planes + q, pl.ds(LEAD + 8 * t, 8)] = tile
    for k in range(7):
        for t in range(ny // 8):
            for q in (0, nx + 1):
                c[k, q, pl.ds(8 * t, 8)] = tile
        for side in range(2):
            for t in range(nx // 8):
                cyrecv[side, k, pl.ds(8 * t, 8)] = tile
    for par in range(2):
        for side in range(2):
            for p in range(np_):
                for t in range(nx // 8):
                    yrecv[par, side, p, 1, pl.ds(8 * t, 8)] = tile

    barrier = pltpu.get_barrier_semaphore()
    for d in range(8):

        @pl.when(to[d])
        def _(d=d):
            pl.semaphore_signal(barrier, inc=1, device_id=where[d], device_id_type=MESH)

    pl.semaphore_wait(barrier, sum(h.astype(jnp.int32) for h in to))

    def copy(d, par, p):
        if d in X_DIRS:
            src = va.at[pl.ds(p * planes + (2 if d == 0 else nx), 2), pl.ds(LEAD, ny)]
            dst = xrecv.at[par, d, p]
        elif d in Y_DIRS:
            src = ysend.at[d - 2, p]
            dst = yrecv.at[par, d - 2, p]
        else:
            src = ksend.at[d - 4, p]
            dst = krecv.at[par, d - 4, p]
        return pltpu.make_async_remote_copy(
            src_ref=src,
            dst_ref=dst,
            send_sem=send_sem.at[d, p],
            recv_sem=recv_sem.at[par, d, p],
            device_id=where[d],
            device_id_type=MESH,
        )

    def copy_coupling(d):
        if d in X_DIRS:
            src = c.at[:, 1 if d == 0 else nx]
            dst = c.at[:, nx + 1 if d == 0 else 0]
        else:
            src, dst = cysend.at[d - 2], cyrecv.at[d - 2]
        return pltpu.make_async_remote_copy(
            src_ref=src,
            dst_ref=dst,
            send_sem=csend_sem.at[d],
            recv_sem=crecv_sem.at[d],
            device_id=where[d],
            device_id_type=MESH,
        )

    def along_x(p, x, y, count):
        return pl.ds((p * planes + x + 2) * rows + LEAD + y, count, stride=rows)

    def start(dirs, par, p):
        for d in dirs:

            @pl.when(to[d])
            def _(d=d):
                copy(d, par, p).start()

    def pack_y(p):
        for side, edge in enumerate(((0, 1), (ny - 1, ny - 2))):
            for n, y in enumerate(edge):
                ysend[side, p, n] = fa[along_x(p, 0, y, nx), :]
        for d in CORNERS:
            sx, sy = DIRECTIONS[d]
            x, y = (0 if sx < 0 else nx - 1), (0 if sy < 0 else ny - 1)
            ksend[d - 4, p] = va[p * planes + x + 2, pl.ds(LEAD + y, 1)]

    def receive(par, p):
        for d in (0, 1, 4, 5, 6, 7, 2, 3):

            @pl.when(from_[d])
            def _(d=d):
                sx, sy = DIRECTIONS[d]
                x, y = (nx if sx < 0 else -1), (ny if sy < 0 else -1)
                copy(d, par, p).wait_recv()
                if d in X_DIRS:
                    for n in range(2):
                        q = p * planes + (nx + 2 if d == 0 else 0) + n
                        va[q, pl.ds(LEAD, ny)] = xrecv[par, d, p, n]
                elif d in Y_DIRS:
                    fa[along_x(p, 0, y, nx), :] = yrecv[par, d - 2, p, 0]
                else:
                    va[p * planes + x + 2, pl.ds(LEAD + y, 1)] = krecv[par, d - 4, p]

    def wait_sent(p):
        for d in range(8):

            @pl.when(to[d])
            def _(d=d):
                copy(d, 0, p).wait_send()

    def first_send(p):
        load(p).wait()
        pack_y(p)
        start((2, 3, 4, 5, 6, 7, 0, 1), 0, p)

    first_send(0)
    for k in range(7):
        load_coupling(k).wait()
    lane = lax.broadcasted_iota(jnp.int32, (8, 128), 1)

    def clip_edges(i, _):
        for t in range(ny // 8):
            at = pl.ds(8 * t, 8)
            c[5, i, at] = jnp.where(lane == 127, 0.0, c[5, i, at])
            c[6, i, at] = jnp.where(lane == 0, 0.0, c[6, i, at])
        return 0

    lax.fori_loop(1, nx + 1, clip_edges, 0)
    for side, y in enumerate((0, ny - 1)):
        for k in range(7):
            cysend[side, k] = fc[pl.ds((k * (nx + 2) + 1) * ny + y, nx, stride=ny), :]
    for d in (2, 3, 0, 1):

        @pl.when(to[d])
        def _(d=d):
            copy_coupling(d).start()

    for p in range(1, np_):
        first_send(p)
    for d in (0, 1, 2, 3):

        @pl.when(from_[d])
        def _(d=d):
            copy_coupling(d).wait_recv()

    def combine(coef, v, ahead, behind, up, down):
        r = coef[0] * v
        r = r + (coef[1] * ahead + coef[2] * behind)
        r = r + (coef[3] * up + coef[4] * down)
        return r + (coef[5] * pltpu.roll(v, 127, 1) + coef[6] * pltpu.roll(v, 1, 1))

    def sweep(src, dst, p, first, count, tiles, unroll):
        def at(x, t, off=0):
            return src[p * planes + x + 2, pl.ds(LEAD + 8 * t + off, 8)]

        def one(x, prev, cur):
            nxt = []
            for n, t in enumerate(tiles):
                coef = [c[k, x + 1, pl.ds(8 * t, 8)] for k in range(7)]
                ahead = at(x + 1, t)
                dst[p * planes + x + 2, pl.ds(LEAD + 8 * t, 8)] = combine(
                    coef, cur[n], ahead, prev[n], at(x, t, 1), at(x, t, -1)
                )
                nxt.append(ahead)
            return cur, tuple(nxt)

        def body(block, carry):
            for u in range(unroll):
                carry = one(first + block * unroll + u, *carry)
            return carry

        init = tuple(at(first - 1, t) for t in tiles), tuple(at(first, t) for t in tiles)
        lax.fori_loop(0, count // unroll, body, init)

    def outer_rows(par, p):
        for side, y in enumerate((ny, -1)):
            inner = along = None
            for t in range(nx // 8):
                coef = [cyrecv[side, k, pl.ds(8 * t, 8)] for k in range(7)]
                v = fa[along_x(p, 8 * t, y, 8), :]
                ahead = fa[along_x(p, 8 * t + 1, y, 8), :]
                behind = fa[along_x(p, 8 * t - 1, y, 8), :]
                inner = fa[along_x(p, 8 * t, ny - 1 if side == 0 else 0, 8), :]
                outer = yrecv[par, side, p, 1, pl.ds(8 * t, 8)]
                up, down = (outer, inner) if side == 0 else (inner, outer)
                fb[along_x(p, 8 * t, y, 8), :] = combine(coef, v, ahead, behind, up, down)

    def save(p):
        return pltpu.make_async_copy(
            va.at[pl.ds(p * planes + 2, nx), pl.ds(LEAD, ny)], out_hbm.at[:, :, pl.ds(p * 128, 128)], load_sem.at[p]
        )

    def work(n, _):
        block, p = n // np_, lax.rem(n, np_)
        par = lax.rem(block, 2)
        receive(par, p)
        sweep(va, vb, p, -1, nx + 2, (0, 1, 2, 3), UNROLL_A)
        outer_rows(par, p)
        wait_sent(p)
        sweep(vb, va, p, 0, nx, (0, 3), UNROLL_B)

        @pl.when(block < blocks - 1)
        def _():
            pack_y(p)
            start((2, 3, 4, 5, 6, 7), 1 - par, p)

        sweep(vb, va, p, 0, nx, (1, 2), UNROLL_B)

        @pl.when(block < blocks - 1)
        def _():
            start((0, 1), 1 - par, p)

        return 0

    lax.fori_loop(0, blocks * np_, work, 0)
    for p in range(np_):
        save(p).start()
    for d in (0, 1, 2, 3):

        @pl.when(to[d])
        def _(d=d):
            copy_coupling(d).wait_send()

    for p in range(np_):
        save(p).wait()


def stencil(probes, coupling):
    np_, nx, ny, nz = probes.shape
    f32 = jnp.float32
    field = pltpu.VMEM((np_ * (nx + 4), ny + 2 * LEAD, nz), f32)
    return pl.pallas_call(
        functools.partial(stencil_kernel, np_, nx, ny),
        out_shape=jax.ShapeDtypeStruct((nx, ny, np_ * nz), f32),
        in_specs=[pl.BlockSpec(memory_space=pltpu.HBM)] * 2,
        out_specs=pl.BlockSpec(memory_space=pl.ANY),
        scratch_shapes=[
            field,
            field,
            pltpu.VMEM((7, nx + 2, ny, nz), f32),
            pltpu.VMEM((2, 7, nx, nz), f32),
            pltpu.VMEM((2, 7, nx, nz), f32),
            pltpu.VMEM((2, 2, np_, 2, ny, nz), f32),
            pltpu.VMEM((2, 2, np_, 2, nx, nz), f32),
            pltpu.VMEM((2, 4, np_, 1, nz), f32),
            pltpu.VMEM((2, np_, 2, nx, nz), f32),
            pltpu.VMEM((4, np_, 1, nz), f32),
            pltpu.SemaphoreType.DMA((np_,)),
            pltpu.SemaphoreType.DMA((7,)),
            pltpu.SemaphoreType.DMA((8, np_)),
            pltpu.SemaphoreType.DMA((2, 8, np_)),
            pltpu.SemaphoreType.DMA((4,)),
            pltpu.SemaphoreType.DMA((4,)),
        ],
        compiler_params=pltpu.CompilerParams(collective_id=0, has_side_effects=True, vmem_limit_bytes=32 << 20),
        name="stencil",
    )(probes, coupling)


def sense_kernel(np_, nx, ny, total_y, field, cell, frac, noise, slot, out, data):
    tx, ty = lax.axis_index("tx"), lax.axis_index("ty")
    lines, lanes = cell.shape
    bf16, f32 = jnp.bfloat16, jnp.float32

    def dot(a, b, dims=((1,), (0,))):
        return lax.dot_general(a, b, (dims, ((), ())), preferred_element_type=f32)

    def split(x):
        high = x.astype(bf16)
        rest = x - high.astype(f32)
        middle = rest.astype(bf16)
        return high, middle, (rest - middle.astype(f32)).astype(bf16)

    shift_z = 128 .bit_length() - 1
    shift_x = shift_z + total_y.bit_length() - 1
    place = cell[...]
    local_x = lax.shift_right_logical(place, shift_x) - tx * nx
    local_y = (lax.shift_right_logical(place, shift_z) & (total_y - 1)) - ty * ny
    inside = (local_x >= 0) & (local_x < nx) & (local_y >= 0) & (local_y < ny)
    ones = jnp.where(inside, 1.0, 0.0)
    count = jnp.sum(ones).astype(jnp.int32)

    def iota(shape, dim):
        return lax.broadcasted_iota(jnp.int32, shape, dim)

    upto = jnp.where(iota((lanes, lanes), 0) <= iota((lanes, lanes), 1), 1.0, 0.0).astype(bf16)
    before = jnp.where(iota((lines, lines), 1) < iota((lines, lines), 0), 1.0, 0.0).astype(bf16)
    marks = ones.astype(bf16)
    within = dot(marks, upto)
    totals = dot(marks, jnp.ones((lanes, lanes), bf16))
    rank = dot(before, totals.astype(bf16)) + within - 1.0
    rank = jnp.where(inside, rank, -1.0).astype(jnp.int32)

    def as_float(x):
        return jnp.where(inside, x, 0).astype(f32)

    parts = [as_float(local_x), as_float(local_y), as_float(place & 127)]
    parts += [lax.shift_right_logical(slot[...], shift_z).astype(f32), (slot[...] & 127).astype(f32)]
    parts += [x.astype(f32) for x in split(frac[...])] + [x.astype(f32) for x in split(noise[...])]
    for k, part in enumerate(parts):
        data[pl.ds(k, lines, stride=16), :] = part
    for k in range(len(parts), 16):
        data[pl.ds(k, lines, stride=16), :] = jnp.zeros((lines, lanes), f32)

    out[...] = jnp.zeros_like(out)
    row_id = iota((CHUNK, lanes), 0)
    lane_id = iota((CHUNK, lanes), 1)

    def chunk(n, _):
        first = n * CHUNK
        picked = jnp.zeros((CHUNK, 16), f32)
        for r in range(lines):
            hot = jnp.where(rank[r : r + 1, :] - first == row_id, 1.0, 0.0).astype(bf16)
            picked = picked + dot(hot, data[pl.ds(16 * r, 16), :].astype(bf16), ((1,), (1,)))

        def column(k):
            return picked[:, k : k + 1]

        line = (column(0) * ny + column(1)).astype(jnp.int32)
        height = column(2).astype(jnp.int32)
        high = column(3).astype(jnp.int32)
        low = column(4).astype(jnp.int32)
        part_up = column(5) + column(6) + column(7)
        variance = column(8) + column(9) + column(10)
        got = jnp.zeros((CHUNK, np_ * 128), f32)
        wide = 128
        for b in range(nx * ny // wide):
            hot = jnp.where(line - b * wide == lane_id, 1.0, 0.0).astype(bf16)
            for piece in split(field[pl.ds(b * wide, wide), :]):
                got = got + dot(hot, piece)
        weight = jnp.where(lane_id == height, 1.0 - part_up, 0.0) + jnp.where(lane_id == height + 1, part_up, 0.0)
        energy = jnp.zeros((CHUNK, 1), f32)
        for p in range(np_):
            value = jnp.sum(got[:, p * 128 : (p + 1) * 128] * weight, axis=1, keepdims=True)
            energy = energy + value * value
        valid = row_id[:, :1] + first < count
        grad = jnp.where(valid, -energy / jnp.where(valid, variance, 1.0), 0.0)
        to_line = jnp.where(iota((CHUNK, lines), 1) == high, 1.0, 0.0)
        to_lane = jnp.where(lane_id == low, grad, 0.0)
        out[...] += lax.dot_general(
            to_line, to_lane, (((0,), (0,)), ((), ())), precision=lax.Precision.HIGHEST, preferred_element_type=f32
        )
        return 0

    lax.fori_loop(0, (count + CHUNK - 1) // CHUNK, chunk, 0)


def sense(field, cell, frac, noise, slot, np_, nx, ny, total_y):
    return pl.pallas_call(
        functools.partial(sense_kernel, np_, nx, ny, total_y),
        out_shape=jax.ShapeDtypeStruct(cell.shape, jnp.float32),
        in_specs=[pl.BlockSpec(memory_space=pltpu.VMEM)] * 5,
        out_specs=pl.BlockSpec(memory_space=pltpu.VMEM),
        scratch_shapes=[pltpu.VMEM((16 * cell.shape[0], cell.shape[1]), jnp.float32)],
        compiler_params=pltpu.CompilerParams(vmem_limit_bytes=32 << 20),
        name="sense",
    )(field, cell, frac, noise, slot)


def collect_kernel(terms, out, first, rows, second, send1, recv1, send2, recv2):
    me, tx, ty = lax.axis_index("probe"), lax.axis_index("tx"), lax.axis_index("ty")
    n, ntx, nty = lax.axis_size("probe"), lax.axis_size("tx"), lax.axis_size("ty")
    probes = [{"probe": lax.rem(me + k, n)} for k in range(n)]
    pairs = [(a, b) for a in range(ntx) for b in range(nty)][1:]

    def tile(a, b):
        return {"tx": lax.rem(tx + a, ntx), "ty": lax.rem(ty + b, nty)}

    barrier = pltpu.get_barrier_semaphore()
    for k in range(1, n):
        pl.semaphore_signal(barrier, inc=1, device_id=probes[k], device_id_type=MESH)
    for a, b in pairs:
        pl.semaphore_signal(barrier, inc=1, device_id=tile(a, b), device_id_type=MESH)
    pl.semaphore_wait(barrier, n - 1 + len(pairs))

    copies = []
    for k in range(1, n):
        cp = pltpu.make_async_remote_copy(
            src_ref=terms.at[pl.ds(pl.multiple_of(lax.rem(me + k, n) * ntx, 8), ntx)],
            dst_ref=first.at[k],
            send_sem=send1.at[k],
            recv_sem=recv1.at[k],
            device_id=probes[k],
            device_id_type=MESH,
        )
        cp.start()
        copies.append(cp)
    total = terms[pl.ds(pl.multiple_of(me * ntx, 8), ntx), :]
    for k in range(1, n):
        copies[k - 1].wait_recv()
        total = total + first[k]
    for a in range(ntx):
        rows[a] = total[a : a + 1, :]
    for a, b in pairs:
        cp = pltpu.make_async_remote_copy(
            src_ref=rows.at[lax.rem(tx + a, ntx)],
            dst_ref=second.at[a * nty + b],
            send_sem=send2.at[a * nty + b],
            recv_sem=recv2.at[a * nty + b],
            device_id=tile(a, b),
            device_id_type=MESH,
        )
        cp.start()
        copies.append(cp)
    mine = rows[tx]
    for cp, (a, b) in zip(copies[n - 1 :], pairs):
        cp.wait_recv()
        mine = mine + second[a * nty + b]
    width = 128 // nty
    result = mine
    for b in range(1, nty):
        result = jnp.where(ty == b, pltpu.roll(mine, 128 - width * b, 1), result)
    out[...] = result[:, :width]
    for cp in copies:
        cp.wait_send()


def collect(terms):
    n, ntx, nty = lax.axis_size("probe"), lax.axis_size("tx"), lax.axis_size("ty")
    return pl.pallas_call(
        collect_kernel,
        out_shape=jax.ShapeDtypeStruct((1, 128 // nty), jnp.float32),
        in_specs=[pl.BlockSpec(memory_space=pltpu.VMEM)],
        out_specs=pl.BlockSpec(memory_space=pltpu.VMEM),
        scratch_shapes=[
            pltpu.VMEM((n, ntx, 128), jnp.float32),
            pltpu.VMEM((ntx, 1, 128), jnp.float32),
            pltpu.VMEM((ntx * nty, 1, 128), jnp.float32),
            pltpu.SemaphoreType.DMA((n,)),
            pltpu.SemaphoreType.DMA((n,)),
            pltpu.SemaphoreType.DMA((ntx * nty,)),
            pltpu.SemaphoreType.DMA((ntx * nty,)),
        ],
        compiler_params=pltpu.CompilerParams(collective_id=1, has_side_effects=True),
        name="collect",
    )(terms)


def shards(probes, coupling, sensor_cell, sensor_frac, noise_var, owner_slot):
    np_, nx, ny, nz = probes.shape
    field = stencil(probes, coupling).reshape(nx * ny, np_ * nz)
    small = [a.reshape(-1, 128) for a in (sensor_cell, sensor_frac, noise_var, owner_slot)]
    terms = sense(field, *small, np_, nx, ny, ny * lax.axis_size("ty"))
    return collect(terms).reshape(-1)


def solution(mesh):
    in_specs = (P("probe", "tx", "ty", None), P(None, "tx", "ty", None), P(), P(), P(), P())
    out_specs = P(("probe", "tx", "ty"))
    return jax.shard_map(shards, mesh=mesh, in_specs=in_specs, out_specs=out_specs, check_vma=False)
```

```python
import functools

import jax
import jax.numpy as jnp
from jax import lax
from jax.experimental import pallas as pl
from jax.experimental.pallas import tpu as pltpu
from jax.sharding import PartitionSpec as P

STEPS = 16
MESH = pl.DeviceIdType.MESH
LEAD = 8
CAPACITY = 288


DIRECTIONS = ((-1, 0), (1, 0), (0, -1), (0, 1), (-1, -1), (-1, 1), (1, -1), (1, 1))
X_DIRS, Y_DIRS, CORNERS = (0, 1), (2, 3), (4, 5, 6, 7)


def stencil_kernel(
    np_, nx, ny, probes_hbm, coup_hbm, out_hbm,
    va, vb, c, cyrecv, cysend, xrecv, yrecv, krecv, ysend, ksend,
    load_sem, coup_sem, send_sem, recv_sem, csend_sem, crecv_sem,
):
    planes = nx + 4
    rows = ny + 2 * LEAD
    blocks = STEPS // 2
    fa, fb = (v.reshape(np_ * planes * rows, 128) for v in (va, vb))
    fc = c.reshape(7 * (nx + 2) * ny, 128)
    tx, ty = lax.axis_index("tx"), lax.axis_index("ty")
    ntx, nty = lax.axis_size("tx"), lax.axis_size("ty")

    def exists(sx, sy):
        return (tx + sx >= 0) & (tx + sx < ntx) & (ty + sy >= 0) & (ty + sy < nty)

    to = [exists(sx, sy) for sx, sy in DIRECTIONS]
    from_ = [exists(-sx, -sy) for sx, sy in DIRECTIONS]
    where = [{"tx": tx + sx, "ty": ty + sy} for sx, sy in DIRECTIONS]

    def load(p):
        return pltpu.make_async_copy(
            probes_hbm.at[p], va.at[pl.ds(p * planes + 2, nx), pl.ds(LEAD, ny)], load_sem.at[p]
        )

    def load_coupling(k):
        return pltpu.make_async_copy(coup_hbm.at[k], c.at[k, pl.ds(1, nx)], coup_sem.at[k])

    load(0).start()
    for k in range(7):
        load_coupling(k).start()
    for p in range(1, np_):
        load(p).start()

    tile = jnp.zeros((8, 128), jnp.float32)

    def zero_field(q, _):
        va[q, pl.ds(0, 8)] = tile
        va[q, pl.ds(LEAD + ny, 8)] = tile
        return 0

    lax.fori_loop(0, np_ * planes, zero_field, 0)
    for p in range(np_):
        for q in (0, 1, nx + 2, nx + 3):
            for t in range(ny // 8):
                va[p * planes + q, pl.ds(LEAD + 8 * t, 8)] = tile
    for k in range(7):
        for t in range(ny // 8):
            for q in (0, nx + 1):
                c[k, q, pl.ds(8 * t, 8)] = tile
        for side in range(2):
            for t in range(nx // 8):
                cyrecv[side, k, pl.ds(8 * t, 8)] = tile
    for par in range(2):
        for side in range(2):
            for p in range(np_):
                for t in range(nx // 8):
                    yrecv[par, side, p, 1, pl.ds(8 * t, 8)] = tile

    barrier = pltpu.get_barrier_semaphore()
    for d in range(8):

        @pl.when(to[d])
        def _(d=d):
            pl.semaphore_signal(barrier, inc=1, device_id=where[d], device_id_type=MESH)

    pl.semaphore_wait(barrier, sum(h.astype(jnp.int32) for h in to))

    def copy(d, par, p):
        if d in X_DIRS:
            src = va.at[pl.ds(p * planes + (2 if d == 0 else nx), 2), pl.ds(LEAD, ny)]
            dst = xrecv.at[par, d, p]
        elif d in Y_DIRS:
            src = ysend.at[d - 2, p]
            dst = yrecv.at[par, d - 2, p]
        else:
            src = ksend.at[d - 4, p]
            dst = krecv.at[par, d - 4, p]
        return pltpu.make_async_remote_copy(
            src_ref=src,
            dst_ref=dst,
            send_sem=send_sem.at[d, p],
            recv_sem=recv_sem.at[par, d, p],
            device_id=where[d],
            device_id_type=MESH,
        )

    def copy_coupling(d):
        if d in X_DIRS:
            src = c.at[:, 1 if d == 0 else nx]
            dst = c.at[:, nx + 1 if d == 0 else 0]
        else:
            src, dst = cysend.at[d - 2], cyrecv.at[d - 2]
        return pltpu.make_async_remote_copy(
            src_ref=src,
            dst_ref=dst,
            send_sem=csend_sem.at[d],
            recv_sem=crecv_sem.at[d],
            device_id=where[d],
            device_id_type=MESH,
        )

    def along_x(p, x, y, count):
        return pl.ds((p * planes + x + 2) * rows + LEAD + y, count, stride=rows)

    def start(dirs, par, p):
        for d in dirs:

            @pl.when(to[d])
            def _(d=d):
                copy(d, par, p).start()

    def pack_y(p):
        for side, edge in enumerate(((0, 1), (ny - 1, ny - 2))):
            for n, y in enumerate(edge):
                ysend[side, p, n] = fa[along_x(p, 0, y, nx), :]
        for d in CORNERS:
            sx, sy = DIRECTIONS[d]
            x, y = (0 if sx < 0 else nx - 1), (0 if sy < 0 else ny - 1)
            ksend[d - 4, p] = va[p * planes + x + 2, pl.ds(LEAD + y, 1)]

    def receive(par, p):
        for d in (0, 1, 4, 5, 6, 7, 2, 3):

            @pl.when(from_[d])
            def _(d=d):
                sx, sy = DIRECTIONS[d]
                x, y = (nx if sx < 0 else -1), (ny if sy < 0 else -1)
                copy(d, par, p).wait_recv()
                if d in X_DIRS:
                    for n in range(2):
                        q = p * planes + (nx + 2 if d == 0 else 0) + n
                        va[q, pl.ds(LEAD, ny)] = xrecv[par, d, p, n]
                elif d in Y_DIRS:
                    fa[along_x(p, 0, y, nx), :] = yrecv[par, d - 2, p, 0]
                else:
                    va[p * planes + x + 2, pl.ds(LEAD + y, 1)] = krecv[par, d - 4, p]

    def wait_sent(p):
        for d in range(8):

            @pl.when(to[d])
            def _(d=d):
                copy(d, 0, p).wait_send()

    def first_send(p):
        load(p).wait()
        pack_y(p)
        start((2, 3, 4, 5, 6, 7, 0, 1), 0, p)

    first_send(0)
    for k in range(7):
        load_coupling(k).wait()
    lane = lax.broadcasted_iota(jnp.int32, (8, 128), 1)

    def clip_edges(i, _):
        for t in range(ny // 8):
            at = pl.ds(8 * t, 8)
            c[5, i, at] = jnp.where(lane == 127, 0.0, c[5, i, at])
            c[6, i, at] = jnp.where(lane == 0, 0.0, c[6, i, at])
        return 0

    lax.fori_loop(1, nx + 1, clip_edges, 0)
    for side, y in enumerate((0, ny - 1)):
        for k in range(7):
            cysend[side, k] = fc[pl.ds((k * (nx + 2) + 1) * ny + y, nx, stride=ny), :]
    for d in (2, 3, 0, 1):

        @pl.when(to[d])
        def _(d=d):
            copy_coupling(d).start()

    for p in range(1, np_):
        first_send(p)
    for d in (0, 1, 2, 3):

        @pl.when(from_[d])
        def _(d=d):
            copy_coupling(d).wait_recv()

    def combine(coef, v, ahead, behind, up, down):
        r = coef[0] * v
        r = r + (coef[1] * ahead + coef[2] * behind)
        r = r + (coef[3] * up + coef[4] * down)
        return r + (coef[5] * pltpu.roll(v, 127, 1) + coef[6] * pltpu.roll(v, 1, 1))

    def sweep(src, dst, p, first, count, tiles):
        def at(x, t, off=0):
            return src[p * planes + x + 2, pl.ds(LEAD + 8 * t + off, 8)]

        def one(x, prev, cur):
            nxt = []
            for n, t in enumerate(tiles):
                coef = [c[k, x + 1, pl.ds(8 * t, 8)] for k in range(7)]
                ahead = at(x + 1, t)
                dst[p * planes + x + 2, pl.ds(LEAD + 8 * t, 8)] = combine(
                    coef, cur[n], ahead, prev[n], at(x, t, 1), at(x, t, -1)
                )
                nxt.append(ahead)
            return cur, tuple(nxt)

        carry = tuple(at(first - 1, t) for t in tiles), tuple(at(first, t) for t in tiles)
        for x in range(first, first + count):
            carry = one(x, *carry)

    def outer_rows(par, p):
        for side, y in enumerate((ny, -1)):
            inner = along = None
            for t in range(nx // 8):
                coef = [cyrecv[side, k, pl.ds(8 * t, 8)] for k in range(7)]
                v = fa[along_x(p, 8 * t, y, 8), :]
                ahead = fa[along_x(p, 8 * t + 1, y, 8), :]
                behind = fa[along_x(p, 8 * t - 1, y, 8), :]
                inner = fa[along_x(p, 8 * t, ny - 1 if side == 0 else 0, 8), :]
                outer = yrecv[par, side, p, 1, pl.ds(8 * t, 8)]
                up, down = (outer, inner) if side == 0 else (inner, outer)
                fb[along_x(p, 8 * t, y, 8), :] = combine(coef, v, ahead, behind, up, down)

    def save(p):
        return pltpu.make_async_copy(
            va.at[pl.ds(p * planes + 2, nx), pl.ds(LEAD, ny)], out_hbm.at[:, :, pl.ds(p * 128, 128)], load_sem.at[p]
        )

    def work(n, _):
        block, p = n // np_, lax.rem(n, np_)
        par = lax.rem(block, 2)
        receive(par, p)
        sweep(va, vb, p, -1, nx + 2, (0, 1, 2, 3))
        outer_rows(par, p)
        wait_sent(p)
        sweep(vb, va, p, 0, nx, (0, 3))

        @pl.when(block < blocks - 1)
        def _():
            pack_y(p)
            start((2, 3, 4, 5, 6, 7), 1 - par, p)

        sweep(vb, va, p, 0, nx, (1, 2))

        @pl.when(block < blocks - 1)
        def _():
            start((0, 1), 1 - par, p)

        return 0

    lax.fori_loop(0, blocks * np_, work, 0)
    for p in range(np_):
        save(p).start()
    for d in (0, 1, 2, 3):

        @pl.when(to[d])
        def _(d=d):
            copy_coupling(d).wait_send()

    for p in range(np_):
        save(p).wait()


def stencil(probes, coupling):
    np_, nx, ny, nz = probes.shape
    f32 = jnp.float32
    field = pltpu.VMEM((np_ * (nx + 4), ny + 2 * LEAD, nz), f32)
    return pl.pallas_call(
        functools.partial(stencil_kernel, np_, nx, ny),
        out_shape=jax.ShapeDtypeStruct((nx, ny, np_ * nz), f32),
        in_specs=[pl.BlockSpec(memory_space=pltpu.HBM)] * 2,
        out_specs=pl.BlockSpec(memory_space=pl.ANY),
        scratch_shapes=[
            field,
            field,
            pltpu.VMEM((7, nx + 2, ny, nz), f32),
            pltpu.VMEM((2, 7, nx, nz), f32),
            pltpu.VMEM((2, 7, nx, nz), f32),
            pltpu.VMEM((2, 2, np_, 2, ny, nz), f32),
            pltpu.VMEM((2, 2, np_, 2, nx, nz), f32),
            pltpu.VMEM((2, 4, np_, 1, nz), f32),
            pltpu.VMEM((2, np_, 2, nx, nz), f32),
            pltpu.VMEM((4, np_, 1, nz), f32),
            pltpu.SemaphoreType.DMA((np_,)),
            pltpu.SemaphoreType.DMA((7,)),
            pltpu.SemaphoreType.DMA((8, np_)),
            pltpu.SemaphoreType.DMA((2, 8, np_)),
            pltpu.SemaphoreType.DMA((4,)),
            pltpu.SemaphoreType.DMA((4,)),
        ],
        compiler_params=pltpu.CompilerParams(collective_id=0, has_side_effects=True, vmem_limit_bytes=56 << 20),
        name="stencil",
    )(probes, coupling)


def sensor_kernel(
    np_, nx, ny, total_y, field, cell, frac, noise, slot,
    out, crowded, data, terms, first, line_terms, second, send1, recv1, send2, recv2,
):
    me, tx, ty = lax.axis_index("probe"), lax.axis_index("tx"), lax.axis_index("ty")
    n, ntx, nty = lax.axis_size("probe"), lax.axis_size("tx"), lax.axis_size("ty")
    peers = [{"probe": lax.rem(me + k, n)} for k in range(n)]
    pairs = [(a, b) for a in range(ntx) for b in range(nty)][1:]

    def owner(a, b):
        return {"tx": lax.rem(tx + a, ntx), "ty": lax.rem(ty + b, nty)}

    barrier = pltpu.get_barrier_semaphore()
    for k in range(1, n):
        pl.semaphore_signal(barrier, inc=1, device_id=peers[k], device_id_type=MESH)
    for a, b in pairs:
        pl.semaphore_signal(barrier, inc=1, device_id=owner(a, b), device_id_type=MESH)

    lines, lanes = cell.shape
    bf16, f32 = jnp.bfloat16, jnp.float32

    def dot(a, b, dims=((1,), (0,)), **kw):
        return lax.dot_general(a, b, (dims, ((), ())), preferred_element_type=f32, **kw)

    def split(x, count):
        pieces = []
        for _ in range(count):
            pieces.append(x.astype(bf16))
            x = x - pieces[-1].astype(f32)
        return pieces

    def iota(shape, dim):
        return lax.broadcasted_iota(jnp.int32, shape, dim)

    shift_z = lanes.bit_length() - 1
    shift_x = shift_z + total_y.bit_length() - 1
    place = cell[...]
    global_x = lax.shift_right_logical(place, shift_x)
    global_y = lax.shift_right_logical(place, shift_z) & (total_y - 1)
    local_x, local_y = global_x - tx * nx, global_y - ty * ny
    inside = (local_x >= 0) & (local_x < nx) & (local_y >= 0) & (local_y < ny)
    marks = jnp.where(inside, 1.0, 0.0).astype(bf16)
    upto = jnp.where(iota((lanes, lanes), 0) <= iota((lanes, lanes), 1), 1.0, 0.0).astype(bf16)
    before = jnp.where(iota((lines, lines), 1) < iota((lines, lines), 0), 1.0, 0.0).astype(bf16)
    within = dot(marks, upto)
    totals = dot(marks, jnp.ones((lanes, lanes), bf16))
    rank = dot(before, totals.astype(bf16)) + within - 1.0
    rank = jnp.where(inside, rank, -1.0).astype(jnp.int32)

    def as_float(x):
        return jnp.where(inside, x, 0).astype(f32)

    parts = [as_float(local_x), as_float(local_y), as_float(place & (lanes - 1)), jnp.where(inside, 1.0, 0.0)]
    parts += [lax.shift_right_logical(slot[...], shift_z).astype(f32), (slot[...] & (lanes - 1)).astype(f32)]
    parts += [x.astype(f32) for x in split(frac[...], 3) + split(noise[...], 3)]
    for k in range(16):
        data[pl.ds(k, lines, stride=16), :] = parts[k] if k < len(parts) else jnp.zeros((lines, lanes), f32)

    row_id = iota((CAPACITY, lanes), 0)
    lane_id = iota((CAPACITY, lanes), 1)
    picked = jnp.zeros((CAPACITY, 16), f32)
    for r in range(lines):
        hot = jnp.where(rank[r : r + 1, :] == row_id, 1.0, 0.0).astype(bf16)
        picked = picked + dot(hot, data[pl.ds(16 * r, 16), :].astype(bf16), ((1,), (1,)))
    local_x, local_y, height, valid, line, lane = (picked[:, k : k + 1].astype(jnp.int32) for k in range(6))
    above = picked[:, 6:7] + picked[:, 7:8] + picked[:, 8:9]
    variance = picked[:, 9:10] + picked[:, 10:11] + picked[:, 11:12]

    got = jnp.zeros((CAPACITY, np_ * lanes), f32)
    at = local_x * ny + local_y
    for b in range(nx * ny // lanes):
        hot = jnp.where(at - b * lanes == lane_id, 1.0, 0.0).astype(bf16)
        for piece in split(field[pl.ds(b * lanes, lanes), :], 2):
            got = got + dot(hot, piece)
    weight = jnp.where(lane_id == height, 1.0 - above, 0.0) + jnp.where(lane_id == height + 1, above, 0.0)
    energy = jnp.zeros((CAPACITY, 1), f32)
    for p in range(np_):
        value = jnp.sum(got[:, p * lanes : (p + 1) * lanes] * weight, axis=1, keepdims=True)
        energy = energy + value * value
    grad = jnp.where(valid > 0, -energy / jnp.where(valid > 0, variance, 1.0), 0.0)
    to_line = jnp.where(iota((CAPACITY, lines), 1) == line, 1.0, 0.0)
    to_lane = jnp.where(lane_id == lane, grad, 0.0)
    terms[...] = dot(to_line, to_lane, ((0,), (0,)), precision=lax.Precision.HIGHEST)

    pl.semaphore_wait(barrier, n - 1 + len(pairs))
    copies = []
    for k in range(1, n):
        cp = pltpu.make_async_remote_copy(
            src_ref=terms.at[pl.ds(pl.multiple_of(lax.rem(me + k, n) * ntx, 8), ntx)],
            dst_ref=first.at[k],
            send_sem=send1.at[k],
            recv_sem=recv1.at[k],
            device_id=peers[k],
            device_id_type=MESH,
        )
        cp.start()
        copies.append(cp)

    region = lax.div(global_x, nx) * nty + lax.div(global_y, ny)
    for r in range(ntx * nty):
        data[r : r + 1, :] = jnp.sum(jnp.where(region == r, 1.0, 0.0), axis=0, keepdims=True)
    most = jnp.max(jnp.sum(data[: ntx * nty, :], axis=1, keepdims=True))
    crowded[0, 0] = (most > CAPACITY).astype(jnp.int32)

    total = terms[pl.ds(pl.multiple_of(me * ntx, 8), ntx), :]
    for k in range(1, n):
        copies[k - 1].wait_recv()
        total = total + first[k]
    for a in range(ntx):
        line_terms[a] = total[a : a + 1, :]
    for a, b in pairs:
        cp = pltpu.make_async_remote_copy(
            src_ref=line_terms.at[lax.rem(tx + a, ntx)],
            dst_ref=second.at[a * nty + b],
            send_sem=send2.at[a * nty + b],
            recv_sem=recv2.at[a * nty + b],
            device_id=owner(a, b),
            device_id_type=MESH,
        )
        cp.start()
        copies.append(cp)
    mine = line_terms[tx]
    for cp, (a, b) in zip(copies[n - 1 :], pairs):
        cp.wait_recv()
        mine = mine + second[a * nty + b]
    width = lanes // nty
    result = mine
    for b in range(1, nty):
        result = jnp.where(ty == b, pltpu.roll(mine, lanes - width * b, 1), result)
    out[...] = result[:, :width]
    for cp in copies:
        cp.wait_send()


def sensors(field, cell, frac, noise, slot, np_, nx, ny, total_y):
    n, ntx, nty = lax.axis_size("probe"), lax.axis_size("tx"), lax.axis_size("ty")
    lines, lanes = cell.shape
    f32 = jnp.float32
    vmem = pl.BlockSpec(memory_space=pltpu.VMEM)
    return pl.pallas_call(
        functools.partial(sensor_kernel, np_, nx, ny, total_y),
        out_shape=(jax.ShapeDtypeStruct((1, lanes // nty), f32), jax.ShapeDtypeStruct((1, 1), jnp.int32)),
        in_specs=[vmem] * 5,
        out_specs=(vmem, pl.BlockSpec(memory_space=pltpu.SMEM)),
        scratch_shapes=[
            pltpu.VMEM((16 * lines, lanes), f32),
            pltpu.VMEM((lines, lanes), f32),
            pltpu.VMEM((n, ntx, lanes), f32),
            pltpu.VMEM((ntx, 1, lanes), f32),
            pltpu.VMEM((ntx * nty, 1, lanes), f32),
            pltpu.SemaphoreType.DMA((n,)),
            pltpu.SemaphoreType.DMA((n,)),
            pltpu.SemaphoreType.DMA((ntx * nty,)),
            pltpu.SemaphoreType.DMA((ntx * nty,)),
        ],
        compiler_params=pltpu.CompilerParams(collective_id=1, has_side_effects=True, vmem_limit_bytes=32 << 20),
        name="sensors",
    )(field, cell, frac, noise, slot)


def sensors_of_any_number(field, cell, frac, noise, slot, np_, nx, ny, total_y):
    cell, frac, noise, slot = (a.reshape(-1) for a in (cell, frac, noise, slot))
    local_x = cell // (total_y * 128) - lax.axis_index("tx") * nx
    local_y = cell // 128 % total_y - lax.axis_index("ty") * ny
    height = cell % 128
    inside = (local_x >= 0) & (local_x < nx) & (local_y >= 0) & (local_y < ny)
    line = jnp.clip(local_x, 0, nx - 1) * ny + jnp.clip(local_y, 0, ny - 1)
    picked = jnp.take(field, line, axis=0).reshape(-1, np_, 128)
    heights = jnp.arange(128, dtype=jnp.int32)[None, :]
    below = jnp.sum(jnp.where((heights == height[:, None])[:, None], picked, 0.0), axis=2)
    above = jnp.sum(jnp.where((heights == height[:, None] + 1)[:, None], picked, 0.0), axis=2)
    values = (1.0 - frac)[:, None] * below + frac[:, None] * above
    terms = jnp.where(inside, -jnp.sum(values * values, axis=1) / noise, 0.0)
    ordered = jnp.zeros_like(terms).at[slot].set(terms)
    return lax.psum_scatter(ordered, ("probe", "tx", "ty"), scatter_dimension=0, tiled=True)


def shards(probes, coupling, sensor_cell, sensor_frac, noise_var, owner_slot):
    np_, nx, ny, nz = probes.shape
    field = stencil(probes, coupling).reshape(nx * ny, np_ * nz)
    small = [a.reshape(-1, 128) for a in (sensor_cell, sensor_frac, noise_var, owner_slot)]
    sizes = (np_, nx, ny, ny * lax.axis_size("ty"))
    gradient, crowded = sensors(field, *small, *sizes)
    return lax.cond(
        crowded[0, 0] > 0,
        lambda: sensors_of_any_number(field, *small, *sizes),
        lambda: gradient.reshape(-1),
    )


def solution(mesh):
    in_specs = (P("probe", "tx", "ty", None), P(None, "tx", "ty", None), P(), P(), P(), P())
    out_specs = P(("probe", "tx", "ty"))
    return jax.shard_map(shards, mesh=mesh, in_specs=in_specs, out_specs=out_specs, check_vma=False)
```

```python
import functools

import jax
import jax.numpy as jnp
from jax import lax
from jax.experimental import pallas as pl
from jax.experimental.pallas import tpu as pltpu
from jax.sharding import PartitionSpec as P

STEPS = 16
MESH = pl.DeviceIdType.MESH
LEAD = 8
CAPACITY = 288


DIRECTIONS = ((-1, 0), (1, 0), (0, -1), (0, 1), (-1, -1), (-1, 1), (1, -1), (1, 1))
X_DIRS, Y_DIRS, CORNERS = (0, 1), (2, 3), (4, 5, 6, 7)


def kernel(
    np_, nx, ny, probes_hbm, coup_hbm, cell, frac, noise, slot,
    out, crowded, out_hbm,
    va, vb, c, cyrecv, cysend, xrecv, yrecv, krecv, ysend, ksend, data, chosen, terms, gathered,
    load_sem, coup_sem, send_sem, recv_sem, csend_sem, crecv_sem, sum_send, sum_recv,
):
    planes = nx + 4
    rows = ny + 2 * LEAD
    blocks = STEPS // 2
    fa, fb = (v.reshape(np_ * planes * rows, 128) for v in (va, vb))
    fc = c.reshape(7 * (nx + 2) * ny, 128)
    me, tx, ty = lax.axis_index("probe"), lax.axis_index("tx"), lax.axis_index("ty")
    n_probe, ntx, nty = lax.axis_size("probe"), lax.axis_size("tx"), lax.axis_size("ty")

    def exists(sx, sy):
        return (tx + sx >= 0) & (tx + sx < ntx) & (ty + sy >= 0) & (ty + sy < nty)

    to = [exists(sx, sy) for sx, sy in DIRECTIONS]
    from_ = [exists(-sx, -sy) for sx, sy in DIRECTIONS]
    where = [{"tx": tx + sx, "ty": ty + sy} for sx, sy in DIRECTIONS]

    def load(p):
        return pltpu.make_async_copy(
            probes_hbm.at[p], va.at[pl.ds(p * planes + 2, nx), pl.ds(LEAD, ny)], load_sem.at[p]
        )

    def load_coupling(k):
        return pltpu.make_async_copy(coup_hbm.at[k], c.at[k, pl.ds(1, nx)], coup_sem.at[k])

    load(0).start()
    for k in range(7):
        load_coupling(k).start()
    for p in range(1, np_):
        load(p).start()

    tile = jnp.zeros((8, 128), jnp.float32)

    for k in range(7):
        for t in range(ny // 8):
            for q in (0, nx + 1):
                c[k, q, pl.ds(8 * t, 8)] = tile
        for side in range(2):
            for t in range(nx // 8):
                cyrecv[side, k, pl.ds(8 * t, 8)] = tile
    for par in range(2):
        for side in range(2):
            for p in range(np_):
                for t in range(nx // 8):
                    yrecv[par, side, p, 1, pl.ds(8 * t, 8)] = tile

    barrier = pltpu.get_barrier_semaphore()
    for d in range(8):

        @pl.when(to[d])
        def _(d=d):
            pl.semaphore_signal(barrier, inc=1, device_id=where[d], device_id_type=MESH)

    for k in range(1, n_probe):
        pl.semaphore_signal(barrier, inc=1, device_id={"probe": lax.rem(me + k, n_probe)}, device_id_type=MESH)

    def zero_field(q, _):
        va[q, pl.ds(0, 8)] = tile
        va[q, pl.ds(LEAD + ny, 8)] = tile
        return 0

    lax.fori_loop(0, np_ * planes, zero_field, 0)
    for p in range(np_):
        for q in (0, 1, nx + 2, nx + 3):
            for t in range(ny // 8):
                va[p * planes + q, pl.ds(LEAD + 8 * t, 8)] = tile
    choose_sensors(nx, ny, nty, ntx, tx, ty, cell, frac, noise, slot, crowded, data, chosen)
    pl.semaphore_wait(barrier, n_probe - 1 + sum(h.astype(jnp.int32) for h in to))

    def copy(d, par, p):
        if d in X_DIRS:
            src = va.at[pl.ds(p * planes + (2 if d == 0 else nx), 2), pl.ds(LEAD, ny)]
            dst = xrecv.at[par, d, p]
        elif d in Y_DIRS:
            src = ysend.at[d - 2, p]
            dst = yrecv.at[par, d - 2, p]
        else:
            src = ksend.at[d - 4, p]
            dst = krecv.at[par, d - 4, p]
        return pltpu.make_async_remote_copy(
            src_ref=src,
            dst_ref=dst,
            send_sem=send_sem.at[d, p],
            recv_sem=recv_sem.at[par, d, p],
            device_id=where[d],
            device_id_type=MESH,
        )

    def copy_coupling(d):
        if d in X_DIRS:
            src = c.at[:, 1 if d == 0 else nx]
            dst = c.at[:, nx + 1 if d == 0 else 0]
        else:
            src, dst = cysend.at[d - 2], cyrecv.at[d - 2]
        return pltpu.make_async_remote_copy(
            src_ref=src,
            dst_ref=dst,
            send_sem=csend_sem.at[d],
            recv_sem=crecv_sem.at[d],
            device_id=where[d],
            device_id_type=MESH,
        )

    def along_x(p, x, y, count):
        return pl.ds((p * planes + x + 2) * rows + LEAD + y, count, stride=rows)

    def start(dirs, par, p):
        for d in dirs:

            @pl.when(to[d])
            def _(d=d):
                copy(d, par, p).start()

    def pack_y(p):
        for side, edge in enumerate(((0, 1), (ny - 1, ny - 2))):
            for n, y in enumerate(edge):
                ysend[side, p, n] = fa[along_x(p, 0, y, nx), :]
        for d in CORNERS:
            sx, sy = DIRECTIONS[d]
            x, y = (0 if sx < 0 else nx - 1), (0 if sy < 0 else ny - 1)
            ksend[d - 4, p] = va[p * planes + x + 2, pl.ds(LEAD + y, 1)]

    def receive(par, p):
        for d in (0, 1, 4, 5, 6, 7, 2, 3):

            @pl.when(from_[d])
            def _(d=d):
                sx, sy = DIRECTIONS[d]
                x, y = (nx if sx < 0 else -1), (ny if sy < 0 else -1)
                copy(d, par, p).wait_recv()
                if d in X_DIRS:
                    for n in range(2):
                        q = p * planes + (nx + 2 if d == 0 else 0) + n
                        va[q, pl.ds(LEAD, ny)] = xrecv[par, d, p, n]
                elif d in Y_DIRS:
                    fa[along_x(p, 0, y, nx), :] = yrecv[par, d - 2, p, 0]
                else:
                    va[p * planes + x + 2, pl.ds(LEAD + y, 1)] = krecv[par, d - 4, p]

    def wait_sent(p):
        for d in range(8):

            @pl.when(to[d])
            def _(d=d):
                copy(d, 0, p).wait_send()

    def first_send(p):
        load(p).wait()
        pack_y(p)
        start((2, 3, 4, 5, 6, 7, 0, 1), 0, p)

    first_send(0)
    for k in range(7):
        load_coupling(k).wait()
    lane = lax.broadcasted_iota(jnp.int32, (8, 128), 1)

    def clip_edges(i, _):
        for t in range(ny // 8):
            at = pl.ds(8 * t, 8)
            c[5, i, at] = jnp.where(lane == 127, 0.0, c[5, i, at])
            c[6, i, at] = jnp.where(lane == 0, 0.0, c[6, i, at])
        return 0

    lax.fori_loop(1, nx + 1, clip_edges, 0)
    for side, y in enumerate((0, ny - 1)):
        for k in range(7):
            cysend[side, k] = fc[pl.ds((k * (nx + 2) + 1) * ny + y, nx, stride=ny), :]
    for d in (2, 3, 0, 1):

        @pl.when(to[d])
        def _(d=d):
            copy_coupling(d).start()

    for p in range(1, np_):
        first_send(p)
    for d in (0, 1, 2, 3):

        @pl.when(from_[d])
        def _(d=d):
            copy_coupling(d).wait_recv()

    def combine(coef, v, ahead, behind, up, down):
        r = coef[0] * v
        r = r + (coef[1] * ahead + coef[2] * behind)
        r = r + (coef[3] * up + coef[4] * down)
        return r + (coef[5] * pltpu.roll(v, 127, 1) + coef[6] * pltpu.roll(v, 1, 1))

    def sweep(src, dst, p, first, count, tiles):
        def at(x, t, off=0):
            return src[p * planes + x + 2, pl.ds(LEAD + 8 * t + off, 8)]

        def one(x, prev, cur):
            nxt = []
            for n, t in enumerate(tiles):
                coef = [c[k, x + 1, pl.ds(8 * t, 8)] for k in range(7)]
                ahead = at(x + 1, t)
                dst[p * planes + x + 2, pl.ds(LEAD + 8 * t, 8)] = combine(
                    coef, cur[n], ahead, prev[n], at(x, t, 1), at(x, t, -1)
                )
                nxt.append(ahead)
            return cur, tuple(nxt)

        carry = tuple(at(first - 1, t) for t in tiles), tuple(at(first, t) for t in tiles)
        for x in range(first, first + count):
            carry = one(x, *carry)

    def outer_rows(par, p):
        for side, y in enumerate((ny, -1)):
            inner = along = None
            for t in range(nx // 8):
                coef = [cyrecv[side, k, pl.ds(8 * t, 8)] for k in range(7)]
                v = fa[along_x(p, 8 * t, y, 8), :]
                ahead = fa[along_x(p, 8 * t + 1, y, 8), :]
                behind = fa[along_x(p, 8 * t - 1, y, 8), :]
                inner = fa[along_x(p, 8 * t, ny - 1 if side == 0 else 0, 8), :]
                outer = yrecv[par, side, p, 1, pl.ds(8 * t, 8)]
                up, down = (outer, inner) if side == 0 else (inner, outer)
                fb[along_x(p, 8 * t, y, 8), :] = combine(coef, v, ahead, behind, up, down)

    def save(p):
        return pltpu.make_async_copy(
            va.at[pl.ds(p * planes + 2, nx), pl.ds(LEAD, ny)], out_hbm.at[:, :, pl.ds(p * 128, 128)], load_sem.at[p]
        )

    def work(n, _):
        block, p = n // np_, lax.rem(n, np_)
        par = lax.rem(block, 2)
        receive(par, p)
        sweep(va, vb, p, -1, nx + 2, (0, 1, 2, 3))
        outer_rows(par, p)
        wait_sent(p)
        sweep(vb, va, p, 0, nx, (0, 3))

        @pl.when(block < blocks - 1)
        def _():
            pack_y(p)
            start((2, 3, 4, 5, 6, 7), 1 - par, p)

        sweep(vb, va, p, 0, nx, (1, 2))

        @pl.when(block < blocks - 1)
        def _():
            start((0, 1), 1 - par, p)

        @pl.when(block == blocks - 1)
        def _():
            save(p).start()

        return 0

    lax.fori_loop(0, blocks * np_, work, 0)

    sensor_terms(np_, nx, ny, planes, va, chosen, terms)
    offsets = [(k, a, b) for k in range(n_probe) for a in range(ntx) for b in range(nty)]
    place = {o: i for i, o in enumerate(offsets)}

    def far(o):
        k, a, b = o
        return min(k, n_probe - k) + min(a, ntx - a) / 2 + min(b, nty - b)

    for o in sorted(offsets[1:], key=far, reverse=True):
        k, a, b = o
        to_probe, to_tx, to_ty = lax.rem(me + k, n_probe), lax.rem(tx + a, ntx), lax.rem(ty + b, nty)
        pltpu.make_async_remote_copy(
            src_ref=terms.at[to_probe * ntx + to_tx],
            dst_ref=gathered.at[place[o]],
            send_sem=sum_send,
            recv_sem=sum_recv,
            device_id={"probe": to_probe, "tx": to_tx, "ty": to_ty},
            device_id_type=MESH,
        ).start()
    gathered[0] = terms[me * ntx + tx]
    for d in (0, 1, 2, 3):

        @pl.when(to[d])
        def _(d=d):
            copy_coupling(d).wait_send()

    for p in range(np_):
        save(p).wait()
    others = gathered.at[pl.ds(1, len(offsets) - 1)]
    every = pltpu.make_async_remote_copy(
        src_ref=others,
        dst_ref=others,
        send_sem=sum_send,
        recv_sem=sum_recv,
        device_id={"probe": lax.rem(me + 1, n_probe)},
        device_id_type=MESH,
    )
    every.wait_recv()
    sums = [gathered[i] for i in range(8)]
    for i in range(8, len(offsets)):
        sums[i % 8] = sums[i % 8] + gathered[i]
    while len(sums) > 1:
        sums = [u + v for u, v in zip(sums[::2], sums[1::2])]
    lanes = cell.shape[1]
    width = lanes // nty
    result = sums[0]
    for b in range(1, nty):
        result = jnp.where(ty == b, pltpu.roll(sums[0], lanes - width * b, 1), result)
    out[...] = result[:, :width]
    every.wait_send()


def dot(a, b, dims=((1,), (0,)), **kw):
    return lax.dot_general(a, b, (dims, ((), ())), preferred_element_type=jnp.float32, **kw)


def split(x, count):
    pieces = []
    for _ in range(count):
        pieces.append(x.astype(jnp.bfloat16))
        x = x - pieces[-1].astype(jnp.float32)
    return pieces


def iota(shape, dim):
    return lax.broadcasted_iota(jnp.int32, shape, dim)


def choose_sensors(nx, ny, nty, ntx, tx, ty, cell, frac, noise, slot, crowded, data, chosen):
    lines, lanes = cell.shape
    bf16, f32 = jnp.bfloat16, jnp.float32
    total_y = ny * nty
    shift_z = lanes.bit_length() - 1
    shift_x = shift_z + total_y.bit_length() - 1
    place = cell[...]
    global_x = lax.shift_right_logical(place, shift_x)
    global_y = lax.shift_right_logical(place, shift_z) & (total_y - 1)
    region = lax.div(global_x, nx) * nty + lax.div(global_y, ny)
    for r in range(ntx * nty):
        data[r : r + 1, :] = jnp.sum(jnp.where(region == r, 1.0, 0.0), axis=0, keepdims=True)
    most = jnp.max(jnp.sum(data[: ntx * nty, :], axis=1, keepdims=True))
    crowded[0, 0] = (most > CAPACITY).astype(jnp.int32)

    local_x, local_y = global_x - tx * nx, global_y - ty * ny
    inside = region == tx * nty + ty
    marks = jnp.where(inside, 1.0, 0.0).astype(bf16)
    upto = jnp.where(iota((lanes, lanes), 0) <= iota((lanes, lanes), 1), 1.0, 0.0).astype(bf16)
    before = jnp.where(iota((lines, lines), 1) < iota((lines, lines), 0), 1.0, 0.0).astype(bf16)
    within = dot(marks, upto)
    totals = dot(marks, jnp.ones((lanes, lanes), bf16))
    rank = dot(before, totals.astype(bf16)) + within - 1.0
    rank = jnp.where(inside, rank, -1.0).astype(jnp.int32)

    def as_float(x):
        return jnp.where(inside, x, 0).astype(f32)

    parts = [as_float(local_x), as_float(local_y), as_float(place & (lanes - 1)), jnp.where(inside, 1.0, 0.0)]
    parts += [lax.shift_right_logical(slot[...], shift_z).astype(f32), (slot[...] & (lanes - 1)).astype(f32)]
    parts += [x.astype(f32) for x in split(frac[...], 3) + split(noise[...], 3)]
    for k in range(16):
        data[pl.ds(k, lines, stride=16), :] = parts[k] if k < len(parts) else jnp.zeros((lines, lanes), f32)
    row_id = iota((CAPACITY, lanes), 0)
    picked = jnp.zeros((CAPACITY, 16), f32)
    for r in range(lines):
        hot = jnp.where(rank[r : r + 1, :] == row_id, 1.0, 0.0).astype(bf16)
        picked = picked + dot(hot, data[pl.ds(16 * r, 16), :].astype(bf16), ((1,), (1,)))
    chosen[...] = picked


def sensor_terms(np_, nx, ny, planes, field, chosen, terms):
    bf16, f32 = jnp.bfloat16, jnp.float32
    lines, _, lanes = terms.shape
    lane_id = iota((CAPACITY, lanes), 1)
    picked = chosen[...]
    local_x, local_y, height, valid, line, lane = (picked[:, k : k + 1].astype(jnp.int32) for k in range(6))
    above = picked[:, 6:7] + picked[:, 7:8] + picked[:, 8:9]
    variance = picked[:, 9:10] + picked[:, 10:11] + picked[:, 11:12]
    got = jnp.zeros((CAPACITY, np_ * lanes), f32)
    at = local_x * ny + local_y
    deep = 2 * lanes
    wide_id = iota((CAPACITY, deep), 1)
    for b in range(nx * ny // deep):
        hot = jnp.where(at - b * deep == wide_id, 1.0, 0.0).astype(bf16)
        count = deep // ny
        cells = [
            field[pl.ds(p * planes + 2 + b * count, count), pl.ds(LEAD, ny)].reshape(deep, lanes) for p in range(np_)
        ]
        for piece in split(jnp.concatenate(cells, axis=1), 2):
            got = got + dot(hot, piece)
    weight = jnp.where(lane_id == height, 1.0 - above, 0.0) + jnp.where(lane_id == height + 1, above, 0.0)
    energy = jnp.zeros((CAPACITY, 1), f32)
    for p in range(np_):
        value = jnp.sum(got[:, p * lanes : (p + 1) * lanes] * weight, axis=1, keepdims=True)
        energy = energy + value * value
    grad = jnp.where(valid > 0, -energy / jnp.where(valid > 0, variance, 1.0), 0.0)
    to_line = jnp.where(iota((CAPACITY, lines), 1) == line, 1.0, 0.0)
    to_lane = jnp.where(lane_id == lane, grad, 0.0)
    ordered = dot(to_line, to_lane, ((0,), (0,)), precision=lax.Precision.HIGHEST)
    for n in range(lines):
        terms[n] = ordered[n : n + 1, :]


def whole(probes, coupling, cell, frac, noise, slot):
    np_, nx, ny, nz = probes.shape
    f32 = jnp.float32
    lines, lanes = cell.shape
    n, ntx, nty = lax.axis_size("probe"), lax.axis_size("tx"), lax.axis_size("ty")
    field = pltpu.VMEM((np_ * (nx + 4), ny + 2 * LEAD, nz), f32)
    vmem = pl.BlockSpec(memory_space=pltpu.VMEM)
    hbm = pl.BlockSpec(memory_space=pltpu.HBM)
    return pl.pallas_call(
        functools.partial(kernel, np_, nx, ny),
        out_shape=(
            jax.ShapeDtypeStruct((1, lanes // nty), f32),
            jax.ShapeDtypeStruct((1, 1), jnp.int32),
            jax.ShapeDtypeStruct((nx, ny, np_ * nz), f32),
        ),
        in_specs=[hbm, hbm, vmem, vmem, vmem, vmem],
        out_specs=(vmem, pl.BlockSpec(memory_space=pltpu.SMEM), hbm),
        scratch_shapes=[
            field,
            field,
            pltpu.VMEM((7, nx + 2, ny, nz), f32),
            pltpu.VMEM((2, 7, nx, nz), f32),
            pltpu.VMEM((2, 7, nx, nz), f32),
            pltpu.VMEM((2, 2, np_, 2, ny, nz), f32),
            pltpu.VMEM((2, 2, np_, 2, nx, nz), f32),
            pltpu.VMEM((2, 4, np_, 1, nz), f32),
            pltpu.VMEM((2, np_, 2, nx, nz), f32),
            pltpu.VMEM((4, np_, 1, nz), f32),
            pltpu.VMEM((16 * lines, lanes), f32),
            pltpu.VMEM((CAPACITY, 16), f32),
            pltpu.VMEM((lines, 1, lanes), f32),
            pltpu.VMEM((n * ntx * nty, 1, lanes), f32),
            pltpu.SemaphoreType.DMA((np_,)),
            pltpu.SemaphoreType.DMA((7,)),
            pltpu.SemaphoreType.DMA((8, np_)),
            pltpu.SemaphoreType.DMA((2, 8, np_)),
            pltpu.SemaphoreType.DMA((4,)),
            pltpu.SemaphoreType.DMA((4,)),
            pltpu.SemaphoreType.DMA,
            pltpu.SemaphoreType.DMA,
        ],
        compiler_params=pltpu.CompilerParams(collective_id=0, has_side_effects=True, vmem_limit_bytes=56 << 20),
        name="stencil",
    )(probes, coupling, cell, frac, noise, slot)


def sensors_of_any_number(field, cell, frac, noise, slot, np_, nx, ny, total_y):
    cell, frac, noise, slot = (a.reshape(-1) for a in (cell, frac, noise, slot))
    local_x = cell // (total_y * 128) - lax.axis_index("tx") * nx
    local_y = cell // 128 % total_y - lax.axis_index("ty") * ny
    height = cell % 128
    inside = (local_x >= 0) & (local_x < nx) & (local_y >= 0) & (local_y < ny)
    line = jnp.clip(local_x, 0, nx - 1) * ny + jnp.clip(local_y, 0, ny - 1)
    picked = jnp.take(field, line, axis=0).reshape(-1, np_, 128)
    heights = jnp.arange(128, dtype=jnp.int32)[None, :]
    below = jnp.sum(jnp.where((heights == height[:, None])[:, None], picked, 0.0), axis=2)
    above = jnp.sum(jnp.where((heights == height[:, None] + 1)[:, None], picked, 0.0), axis=2)
    values = (1.0 - frac)[:, None] * below + frac[:, None] * above
    terms = jnp.where(inside, -jnp.sum(values * values, axis=1) / noise, 0.0)
    ordered = jnp.zeros_like(terms).at[slot].set(terms)
    return lax.psum_scatter(ordered, ("probe", "tx", "ty"), scatter_dimension=0, tiled=True)


def shards(probes, coupling, sensor_cell, sensor_frac, noise_var, owner_slot):
    np_, nx, ny, nz = probes.shape
    small = [a.reshape(-1, 128) for a in (sensor_cell, sensor_frac, noise_var, owner_slot)]
    gradient, crowded, field = whole(probes, coupling, *small)
    sizes = (np_, nx, ny, ny * lax.axis_size("ty"))
    return lax.cond(
        crowded[0, 0] > 0,
        lambda: sensors_of_any_number(field.reshape(nx * ny, np_ * nz), *small, *sizes),
        lambda: gradient.reshape(-1),
    )


def solution(mesh):
    in_specs = (P("probe", "tx", "ty", None), P(None, "tx", "ty", None), P(), P(), P(), P())
    out_specs = P(("probe", "tx", "ty"))
    return jax.shard_map(shards, mesh=mesh, in_specs=in_specs, out_specs=out_specs, check_vma=False)
```

```python
import functools

import jax
import jax.numpy as jnp
from jax import lax
from jax.experimental import pallas as pl
from jax.experimental.pallas import tpu as pltpu
from jax.sharding import PartitionSpec as P

STEPS = 16
MESH = pl.DeviceIdType.MESH
LEAD = 8
CAPACITY = 288


DIRECTIONS = ((-1, 0), (1, 0), (0, -1), (0, 1), (-1, -1), (-1, 1), (1, -1), (1, 1))
X_DIRS, Y_DIRS, CORNERS = (0, 1), (2, 3), (4, 5, 6, 7)


def kernel(
    np_, nx, ny, probes_hbm, coup_hbm, cell, frac, noise, slot,
    out, crowded,
    va, vb, c, cyrecv, cysend, xrecv, yrecv, krecv, ysend, ksend, data, chosen, hot, weight, energy, terms, gathered,
    load_sem, coup_sem, send_sem, recv_sem, csend_sem, crecv_sem, sum_send, sum_recv,
):
    planes = nx + 4
    rows = ny + 2 * LEAD
    blocks = STEPS // 2
    fa, fb = (v.reshape(np_ * planes * rows, 128) for v in (va, vb))
    fc = c.reshape(7 * (nx + 2) * ny, 128)
    me, tx, ty = lax.axis_index("probe"), lax.axis_index("tx"), lax.axis_index("ty")
    n_probe, ntx, nty = lax.axis_size("probe"), lax.axis_size("tx"), lax.axis_size("ty")

    def exists(sx, sy):
        return (tx + sx >= 0) & (tx + sx < ntx) & (ty + sy >= 0) & (ty + sy < nty)

    to = [exists(sx, sy) for sx, sy in DIRECTIONS]
    from_ = [exists(-sx, -sy) for sx, sy in DIRECTIONS]
    where = [{"tx": tx + sx, "ty": ty + sy} for sx, sy in DIRECTIONS]

    def load(p):
        return pltpu.make_async_copy(
            probes_hbm.at[p], va.at[pl.ds(p * planes + 2, nx), pl.ds(LEAD, ny)], load_sem.at[p]
        )

    def load_coupling(k):
        return pltpu.make_async_copy(coup_hbm.at[k], c.at[k, pl.ds(1, nx)], coup_sem.at[k])

    load(0).start()
    for k in range(7):
        load_coupling(k).start()
    for p in range(1, np_):
        load(p).start()

    tile = jnp.zeros((8, 128), jnp.float32)

    for k in range(7):
        for t in range(ny // 8):
            for q in (0, nx + 1):
                c[k, q, pl.ds(8 * t, 8)] = tile
        for side in range(2):
            for t in range(nx // 8):
                cyrecv[side, k, pl.ds(8 * t, 8)] = tile
    for par in range(2):
        for side in range(2):
            for p in range(np_):
                for t in range(nx // 8):
                    yrecv[par, side, p, 1, pl.ds(8 * t, 8)] = tile

    barrier = pltpu.get_barrier_semaphore()
    for d in range(8):

        @pl.when(to[d])
        def _(d=d):
            pl.semaphore_signal(barrier, inc=1, device_id=where[d], device_id_type=MESH)

    for k in range(1, n_probe):
        pl.semaphore_signal(barrier, inc=1, device_id={"probe": lax.rem(me + k, n_probe)}, device_id_type=MESH)

    def zero_field(q, _):
        va[q, pl.ds(0, 8)] = tile
        va[q, pl.ds(LEAD + ny, 8)] = tile
        return 0

    lax.fori_loop(0, np_ * planes, zero_field, 0)
    for p in range(np_):
        for q in (0, 1, nx + 2, nx + 3):
            for t in range(ny // 8):
                va[p * planes + q, pl.ds(LEAD + 8 * t, 8)] = tile
    pl.semaphore_wait(barrier, n_probe - 1 + sum(h.astype(jnp.int32) for h in to))

    def copy(d, par, p):
        if d in X_DIRS:
            src = va.at[pl.ds(p * planes + (2 if d == 0 else nx), 2), pl.ds(LEAD, ny)]
            dst = xrecv.at[par, d, p]
        elif d in Y_DIRS:
            src = ysend.at[d - 2, p]
            dst = yrecv.at[par, d - 2, p]
        else:
            src = ksend.at[d - 4, p]
            dst = krecv.at[par, d - 4, p]
        return pltpu.make_async_remote_copy(
            src_ref=src,
            dst_ref=dst,
            send_sem=send_sem.at[d, p],
            recv_sem=recv_sem.at[par, d, p],
            device_id=where[d],
            device_id_type=MESH,
        )

    def copy_coupling(d):
        if d in X_DIRS:
            src = c.at[:, 1 if d == 0 else nx]
            dst = c.at[:, nx + 1 if d == 0 else 0]
        else:
            src, dst = cysend.at[d - 2], cyrecv.at[d - 2]
        return pltpu.make_async_remote_copy(
            src_ref=src,
            dst_ref=dst,
            send_sem=csend_sem.at[d],
            recv_sem=crecv_sem.at[d],
            device_id=where[d],
            device_id_type=MESH,
        )

    def along_x(p, x, y, count):
        return pl.ds((p * planes + x + 2) * rows + LEAD + y, count, stride=rows)

    def start(dirs, par, p):
        for d in dirs:

            @pl.when(to[d])
            def _(d=d):
                copy(d, par, p).start()

    def pack_y(p):
        for side, edge in enumerate(((0, 1), (ny - 1, ny - 2))):
            for n, y in enumerate(edge):
                ysend[side, p, n] = fa[along_x(p, 0, y, nx), :]
        for d in CORNERS:
            sx, sy = DIRECTIONS[d]
            x, y = (0 if sx < 0 else nx - 1), (0 if sy < 0 else ny - 1)
            ksend[d - 4, p] = va[p * planes + x + 2, pl.ds(LEAD + y, 1)]

    def receive(par, p):
        for d in (0, 1, 4, 5, 6, 7, 2, 3):

            @pl.when(from_[d])
            def _(d=d):
                sx, sy = DIRECTIONS[d]
                x, y = (nx if sx < 0 else -1), (ny if sy < 0 else -1)
                copy(d, par, p).wait_recv()
                if d in X_DIRS:
                    for n in range(2):
                        q = p * planes + (nx + 2 if d == 0 else 0) + n
                        va[q, pl.ds(LEAD, ny)] = xrecv[par, d, p, n]
                elif d in Y_DIRS:
                    fa[along_x(p, 0, y, nx), :] = yrecv[par, d - 2, p, 0]
                else:
                    va[p * planes + x + 2, pl.ds(LEAD + y, 1)] = krecv[par, d - 4, p]

    def wait_sent(p):
        for d in range(8):

            @pl.when(to[d])
            def _(d=d):
                copy(d, 0, p).wait_send()

    def first_send(p):
        load(p).wait()
        pack_y(p)
        start((2, 3, 4, 5, 6, 7, 0, 1), 0, p)

    first_send(0)
    for k in range(7):
        load_coupling(k).wait()
    lane = lax.broadcasted_iota(jnp.int32, (8, 128), 1)

    def clip_edges(i, _):
        for t in range(ny // 8):
            at = pl.ds(8 * t, 8)
            c[5, i, at] = jnp.where(lane == 127, 0.0, c[5, i, at])
            c[6, i, at] = jnp.where(lane == 0, 0.0, c[6, i, at])
        return 0

    lax.fori_loop(1, nx + 1, clip_edges, 0)
    for side, y in enumerate((0, ny - 1)):
        for k in range(7):
            cysend[side, k] = fc[pl.ds((k * (nx + 2) + 1) * ny + y, nx, stride=ny), :]
    for d in (2, 3, 0, 1):

        @pl.when(to[d])
        def _(d=d):
            copy_coupling(d).start()

    for p in range(1, np_):
        first_send(p)
    choose_sensors(nx, ny, nty, ntx, tx, ty, cell, frac, noise, slot, crowded, data, chosen, hot, weight, energy)
    for d in (0, 1, 2, 3):

        @pl.when(from_[d])
        def _(d=d):
            copy_coupling(d).wait_recv()

    def combine(coef, v, ahead, behind, up, down):
        r = coef[0] * v
        r = r + (coef[1] * ahead + coef[2] * behind)
        r = r + (coef[3] * up + coef[4] * down)
        return r + (coef[5] * pltpu.roll(v, 127, 1) + coef[6] * pltpu.roll(v, 1, 1))

    def sweep(src, dst, p, first, count, tiles):
        def at(x, t, off=0):
            return src[p * planes + x + 2, pl.ds(LEAD + 8 * t + off, 8)]

        def one(x, prev, cur):
            nxt = []
            for n, t in enumerate(tiles):
                coef = [c[k, x + 1, pl.ds(8 * t, 8)] for k in range(7)]
                ahead = at(x + 1, t)
                dst[p * planes + x + 2, pl.ds(LEAD + 8 * t, 8)] = combine(
                    coef, cur[n], ahead, prev[n], at(x, t, 1), at(x, t, -1)
                )
                nxt.append(ahead)
            return cur, tuple(nxt)

        carry = tuple(at(first - 1, t) for t in tiles), tuple(at(first, t) for t in tiles)
        for x in range(first, first + count):
            carry = one(x, *carry)

    def outer_rows(par, p):
        for side, y in enumerate((ny, -1)):
            inner = along = None
            for t in range(nx // 8):
                coef = [cyrecv[side, k, pl.ds(8 * t, 8)] for k in range(7)]
                v = fa[along_x(p, 8 * t, y, 8), :]
                ahead = fa[along_x(p, 8 * t + 1, y, 8), :]
                behind = fa[along_x(p, 8 * t - 1, y, 8), :]
                inner = fa[along_x(p, 8 * t, ny - 1 if side == 0 else 0, 8), :]
                outer = yrecv[par, side, p, 1, pl.ds(8 * t, 8)]
                up, down = (outer, inner) if side == 0 else (inner, outer)
                fb[along_x(p, 8 * t, y, 8), :] = combine(coef, v, ahead, behind, up, down)

    def work(block, _):
        for p in range(np_):
            work_on(block, p)
        return 0

    def work_on(block, p):
        par = lax.rem(block, 2)
        receive(par, p)
        wait_sent(p)
        sweep(va, vb, p, -1, nx + 2, (0, 1, 2, 3))
        outer_rows(par, p)
        sweep(vb, va, p, 0, nx, (0, 3))

        @pl.when(block < blocks - 1)
        def _():
            pack_y(p)
            start((2, 3, 4, 5, 6, 7), 1 - par, p)

        sweep(vb, va, p, 0, nx, (1, 2))

        @pl.when(block < blocks - 1)
        def _():
            start((0, 1), 1 - par, p)

        @pl.when(block == blocks - 1)
        def _():
            add_energy(nx, ny, p * planes + 2, va, hot, weight, energy)

    lax.fori_loop(0, blocks, work, 0)

    sensor_terms(chosen, energy, terms)
    offsets = [(k, a, b) for k in range(n_probe) for a in range(ntx) for b in range(nty)]
    place = {o: i for i, o in enumerate(offsets)}

    def far(o):
        k, a, b = o
        return min(k, n_probe - k) + min(a, ntx - a) / 2 + min(b, nty - b)

    for o in sorted(offsets[1:], key=far, reverse=True):
        k, a, b = o
        to_probe, to_tx, to_ty = lax.rem(me + k, n_probe), lax.rem(tx + a, ntx), lax.rem(ty + b, nty)
        pltpu.make_async_remote_copy(
            src_ref=terms.at[to_probe * ntx + to_tx],
            dst_ref=gathered.at[place[o]],
            send_sem=sum_send,
            recv_sem=sum_recv,
            device_id={"probe": to_probe, "tx": to_tx, "ty": to_ty},
            device_id_type=MESH,
        ).start()
    gathered[0] = terms[me * ntx + tx]
    for d in (0, 1, 2, 3):

        @pl.when(to[d])
        def _(d=d):
            copy_coupling(d).wait_send()

    others = gathered.at[pl.ds(1, len(offsets) - 1)]
    every = pltpu.make_async_remote_copy(
        src_ref=others,
        dst_ref=others,
        send_sem=sum_send,
        recv_sem=sum_recv,
        device_id={"probe": lax.rem(me + 1, n_probe)},
        device_id_type=MESH,
    )
    every.wait_recv()
    sums = [gathered[i] for i in range(8)]
    for i in range(8, len(offsets)):
        sums[i % 8] = sums[i % 8] + gathered[i]
    while len(sums) > 1:
        sums = [u + v for u, v in zip(sums[::2], sums[1::2])]
    lanes = cell.shape[1]
    width = lanes // nty
    result = sums[0]
    for b in range(1, nty):
        result = jnp.where(ty == b, pltpu.roll(sums[0], lanes - width * b, 1), result)
    out[...] = result[:, :width]
    every.wait_send()


def dot(a, b, dims=((1,), (0,)), **kw):
    return lax.dot_general(a, b, (dims, ((), ())), preferred_element_type=jnp.float32, **kw)


def split(x, count):
    pieces = []
    for _ in range(count):
        pieces.append(x.astype(jnp.bfloat16))
        x = x - pieces[-1].astype(jnp.float32)
    return pieces


def iota(shape, dim):
    return lax.broadcasted_iota(jnp.int32, shape, dim)


def choose_sensors(nx, ny, nty, ntx, tx, ty, cell, frac, noise, slot, crowded, data, chosen, hot, weight, energy):
    lines, lanes = cell.shape
    bf16, f32 = jnp.bfloat16, jnp.float32
    total_y = ny * nty
    shift_z = lanes.bit_length() - 1
    shift_x = shift_z + total_y.bit_length() - 1
    place = cell[...]
    global_x = lax.shift_right_logical(place, shift_x)
    global_y = lax.shift_right_logical(place, shift_z) & (total_y - 1)
    region = lax.div(global_x, nx) * nty + lax.div(global_y, ny)
    for r in range(ntx * nty):
        data[r : r + 1, :] = jnp.sum(jnp.where(region == r, 1.0, 0.0), axis=0, keepdims=True)
    most = jnp.max(jnp.sum(data[: ntx * nty, :], axis=1, keepdims=True))
    crowded[0, 0] = (most > CAPACITY).astype(jnp.int32)

    local_x, local_y = global_x - tx * nx, global_y - ty * ny
    inside = region == tx * nty + ty
    marks = jnp.where(inside, 1.0, 0.0).astype(bf16)
    upto = jnp.where(iota((lanes, lanes), 0) <= iota((lanes, lanes), 1), 1.0, 0.0).astype(bf16)
    before = jnp.where(iota((lines, lines), 1) < iota((lines, lines), 0), 1.0, 0.0).astype(bf16)
    within = dot(marks, upto)
    totals = dot(marks, jnp.ones((lanes, lanes), bf16))
    rank = dot(before, totals.astype(bf16)) + within - 1.0
    rank = jnp.where(inside, rank, -1.0).astype(jnp.int32)

    def as_float(x):
        return jnp.where(inside, x, 0).astype(f32)

    parts = [as_float(local_x), as_float(local_y), as_float(place & (lanes - 1)), jnp.where(inside, 1.0, 0.0)]
    parts += [lax.shift_right_logical(slot[...], shift_z).astype(f32), (slot[...] & (lanes - 1)).astype(f32)]
    parts += [x.astype(f32) for x in split(frac[...], 3) + split(noise[...], 3)]
    for k in range(16):
        data[pl.ds(k, lines, stride=16), :] = parts[k] if k < len(parts) else jnp.zeros((lines, lanes), f32)
    row_id = iota((CAPACITY, lanes), 0)
    picked = jnp.zeros((CAPACITY, 16), f32)
    for r in range(lines):
        one = jnp.where(rank[r : r + 1, :] == row_id, 1.0, 0.0).astype(bf16)
        picked = picked + dot(one, data[pl.ds(16 * r, 16), :].astype(bf16), ((1,), (1,)))
    chosen[...] = picked
    line = (picked[:, 0:1] * ny + picked[:, 1:2]).astype(jnp.int32)
    lane_id = iota((CAPACITY, lanes), 1)
    for b in range(nx * ny // lanes):
        hot[:, b * lanes : (b + 1) * lanes] = jnp.where(line - b * lanes == lane_id, 1.0, 0.0).astype(bf16)
    height = picked[:, 2:3].astype(jnp.int32)
    above = picked[:, 6:7] + picked[:, 7:8] + picked[:, 8:9]
    weight[...] = jnp.where(lane_id == height, 1.0 - above, 0.0) + jnp.where(lane_id == height + 1, above, 0.0)
    energy[...] = jnp.zeros_like(energy)


def add_energy(nx, ny, first, field, hot, weight, energy):
    lanes = field.shape[2]
    deep = 2 * lanes
    count = deep // ny
    got = jnp.zeros((CAPACITY, lanes), jnp.float32)
    for b in range(nx * ny // deep):
        cells = field[pl.ds(first + b * count, count), pl.ds(LEAD, ny)].reshape(deep, lanes)
        for piece in split(cells, 2):
            got = got + dot(hot[:, b * deep : (b + 1) * deep], piece)
    value = jnp.sum(got * weight[...], axis=1, keepdims=True)
    energy[...] += value * value


def sensor_terms(chosen, energy, terms):
    lines, _, lanes = terms.shape
    picked = chosen[...]
    valid, line, lane = (picked[:, k : k + 1].astype(jnp.int32) for k in (3, 4, 5))
    variance = picked[:, 9:10] + picked[:, 10:11] + picked[:, 11:12]
    grad = jnp.where(valid > 0, -energy[...] / jnp.where(valid > 0, variance, 1.0), 0.0)
    to_line = jnp.where(iota((CAPACITY, lines), 1) == line, 1.0, 0.0)
    to_lane = jnp.where(iota((CAPACITY, lanes), 1) == lane, grad, 0.0)
    ordered = dot(to_line, to_lane, ((0,), (0,)), precision=lax.Precision.HIGHEST)
    for n in range(lines):
        terms[n] = ordered[n : n + 1, :]


def whole(probes, coupling, cell, frac, noise, slot):
    np_, nx, ny, nz = probes.shape
    f32 = jnp.float32
    lines, lanes = cell.shape
    n, ntx, nty = lax.axis_size("probe"), lax.axis_size("tx"), lax.axis_size("ty")
    field = pltpu.VMEM((np_ * (nx + 4), ny + 2 * LEAD, nz), f32)
    vmem = pl.BlockSpec(memory_space=pltpu.VMEM)
    hbm = pl.BlockSpec(memory_space=pltpu.HBM)
    return pl.pallas_call(
        functools.partial(kernel, np_, nx, ny),
        out_shape=(
            jax.ShapeDtypeStruct((1, lanes // nty), f32),
            jax.ShapeDtypeStruct((1, 1), jnp.int32),
        ),
        in_specs=[hbm, hbm, vmem, vmem, vmem, vmem],
        out_specs=(vmem, pl.BlockSpec(memory_space=pltpu.SMEM)),
        scratch_shapes=[
            field,
            field,
            pltpu.VMEM((7, nx + 2, ny, nz), f32),
            pltpu.VMEM((2, 7, nx, nz), f32),
            pltpu.VMEM((2, 7, nx, nz), f32),
            pltpu.VMEM((2, 2, np_, 2, ny, nz), f32),
            pltpu.VMEM((2, 2, np_, 2, nx, nz), f32),
            pltpu.VMEM((2, 4, np_, 1, nz), f32),
            pltpu.VMEM((2, np_, 2, nx, nz), f32),
            pltpu.VMEM((4, np_, 1, nz), f32),
            pltpu.VMEM((16 * lines, lanes), f32),
            pltpu.VMEM((CAPACITY, 16), f32),
            pltpu.VMEM((CAPACITY, nx * ny), jnp.bfloat16),
            pltpu.VMEM((CAPACITY, lanes), f32),
            pltpu.VMEM((CAPACITY, 1), f32),
            pltpu.VMEM((lines, 1, lanes), f32),
            pltpu.VMEM((n * ntx * nty, 1, lanes), f32),
            pltpu.SemaphoreType.DMA((np_,)),
            pltpu.SemaphoreType.DMA((7,)),
            pltpu.SemaphoreType.DMA((8, np_)),
            pltpu.SemaphoreType.DMA((2, 8, np_)),
            pltpu.SemaphoreType.DMA((4,)),
            pltpu.SemaphoreType.DMA((4,)),
            pltpu.SemaphoreType.DMA,
            pltpu.SemaphoreType.DMA,
        ],
        compiler_params=pltpu.CompilerParams(collective_id=0, has_side_effects=True, vmem_limit_bytes=67_000_000),
        name="stencil",
    )(probes, coupling, cell, frac, noise, slot)


def general(probes, coupling, cell, frac, noise, slot):
    np_, nx, ny, nz = probes.shape

    def neighbour(block, axis, dim, step):
        count = lax.axis_size(axis)
        size = block.shape[dim]
        edge = lax.slice_in_dim(block, 0, 1, axis=dim) if step > 0 else lax.slice_in_dim(block, size - 1, size, axis=dim)
        edge = lax.ppermute(edge, axis, [(i, i - step) for i in range(count) if 0 <= i - step < count])
        if step > 0:
            return jnp.concatenate([lax.slice_in_dim(block, 1, None, axis=dim), edge], axis=dim)
        return jnp.concatenate([edge, lax.slice_in_dim(block, 0, size - 1, axis=dim)], axis=dim)

    def advance(_, v):
        deep = jnp.pad(v, ((0, 0), (0, 0), (0, 0), (1, 1)))
        r = coupling[0] * v
        r = r + coupling[1] * neighbour(v, "tx", 1, 1) + coupling[2] * neighbour(v, "tx", 1, -1)
        r = r + coupling[3] * neighbour(v, "ty", 2, 1) + coupling[4] * neighbour(v, "ty", 2, -1)
        return r + coupling[5] * deep[..., 2:] + coupling[6] * deep[..., :-2]

    field = lax.fori_loop(1, STEPS, advance, advance(0, probes)).reshape(np_, nx * ny, nz)
    total_y = ny * lax.axis_size("ty")
    local_x = cell // (total_y * nz) - lax.axis_index("tx") * nx
    local_y = cell // nz % total_y - lax.axis_index("ty") * ny
    height = (cell % nz)[:, None]
    inside = (local_x >= 0) & (local_x < nx) & (local_y >= 0) & (local_y < ny)
    line = jnp.clip(local_x, 0, nx - 1) * ny + jnp.clip(local_y, 0, ny - 1)
    heights = jnp.arange(nz, dtype=jnp.int32)[None, :]

    def energy(p, total):
        picked = jnp.take(field[p], line, axis=0)
        below = jnp.sum(jnp.where(heights == height, picked, 0.0), axis=1)
        above = jnp.sum(jnp.where(heights == height + 1, picked, 0.0), axis=1)
        value = (1.0 - frac) * below + frac * above
        return total + value * value

    energies = lax.fori_loop(0, np_, energy, jnp.zeros_like(frac))
    terms = jnp.where(inside, -energies / noise, 0.0)
    ordered = jnp.zeros_like(terms).at[slot].set(terms)
    return lax.psum_scatter(ordered, ("probe", "tx", "ty"), scatter_dimension=0, tiled=True)


def shards(probes, coupling, sensor_cell, sensor_frac, noise_var, owner_slot):
    numbers = (sensor_cell, sensor_frac, noise_var, owner_slot)
    gradient, crowded = whole(probes, coupling, *(a.reshape(-1, 128) for a in numbers))
    return lax.cond(crowded[0, 0] > 0, lambda: general(probes, coupling, *numbers), lambda: gradient.reshape(-1))


def solution(mesh):
    in_specs = (P("probe", "tx", "ty", None), P(None, "tx", "ty", None), P(), P(), P(), P())
    out_specs = P(("probe", "tx", "ty"))
    return jax.shard_map(shards, mesh=mesh, in_specs=in_specs, out_specs=out_specs, check_vma=False)
```

```python
import functools

import jax
import jax.numpy as jnp
from jax import lax
from jax.experimental import pallas as pl
from jax.experimental.pallas import tpu as pltpu
from jax.sharding import PartitionSpec as P

STEPS = 16
MESH = pl.DeviceIdType.MESH
LEAD = 8
CAPACITY = 288


DIRECTIONS = ((-1, 0), (1, 0), (0, -1), (0, 1), (-1, -1), (-1, 1), (1, -1), (1, 1))
X_DIRS, Y_DIRS, CORNERS = (0, 1), (2, 3), (4, 5, 6, 7)


def kernel(
    np_, nx, ny, probes_hbm, coup_hbm, cell, frac, noise, slot,
    out, crowded,
    va, vb, c, cyrecv, cysend, xrecv, yrecv, krecv, ysend, ksend, data, chosen, hot, weight, energy, terms, gathered,
    load_sem, coup_sem, send_sem, recv_sem, csend_sem, crecv_sem, sum_send, sum_recv,
):
    planes = nx + 4
    rows = ny + 2 * LEAD
    blocks = STEPS // 2
    fa, fb = (v.reshape(np_ * planes * rows, 128) for v in (va, vb))
    fc = c.reshape(7 * (nx + 2) * ny, 128)
    me, tx, ty = lax.axis_index("probe"), lax.axis_index("tx"), lax.axis_index("ty")
    n_probe, ntx, nty = lax.axis_size("probe"), lax.axis_size("tx"), lax.axis_size("ty")

    def exists(sx, sy):
        return (tx + sx >= 0) & (tx + sx < ntx) & (ty + sy >= 0) & (ty + sy < nty)

    to = [exists(sx, sy) for sx, sy in DIRECTIONS]
    from_ = [exists(-sx, -sy) for sx, sy in DIRECTIONS]
    where = [{"tx": tx + sx, "ty": ty + sy} for sx, sy in DIRECTIONS]

    def load(p):
        return pltpu.make_async_copy(
            probes_hbm.at[p], va.at[pl.ds(p * planes + 2, nx), pl.ds(LEAD, ny)], load_sem.at[p]
        )

    def all_coupling():
        return pltpu.make_async_copy(coup_hbm, c.at[:, pl.ds(1, nx)], coup_sem)

    barrier = pltpu.get_barrier_semaphore()
    for d in range(8):

        @pl.when(to[d])
        def _(d=d):
            pl.semaphore_signal(barrier, inc=1, device_id=where[d], device_id_type=MESH)

    for k in range(1, n_probe):
        pl.semaphore_signal(barrier, inc=1, device_id={"probe": lax.rem(me + k, n_probe)}, device_id_type=MESH)

    load(0).start()
    all_coupling().start()
    for p in range(1, np_):
        load(p).start()

    tile = jnp.zeros((8, 128), jnp.float32)
    for d in X_DIRS:

        @pl.when(jnp.logical_not(from_[d]))
        def _(d=d):
            for k in range(7):
                for t in range(ny // 8):
                    c[k, nx + 1 if d == 0 else 0, pl.ds(8 * t, 8)] = tile

    for d in Y_DIRS:

        @pl.when(jnp.logical_not(from_[d]))
        def _(d=d):
            for t in range(nx // 8):
                for k in range(7):
                    cyrecv[d - 2, k, pl.ds(8 * t, 8)] = tile
                for par in range(2):
                    for p in range(np_):
                        yrecv[par, d - 2, p, 1, pl.ds(8 * t, 8)] = tile

    def zero_field(q, _):
        va[q, pl.ds(0, 8)] = tile
        va[q, pl.ds(LEAD + ny, 8)] = tile
        return 0

    lax.fori_loop(0, np_ * planes, zero_field, 0)
    for p in range(np_):
        for q in (0, 1, nx + 2, nx + 3):
            for t in range(ny // 8):
                va[p * planes + q, pl.ds(LEAD + 8 * t, 8)] = tile
    pl.semaphore_wait(barrier, n_probe - 1 + sum(h.astype(jnp.int32) for h in to))

    def copy(d, par, p):
        if d in X_DIRS:
            src = va.at[pl.ds(p * planes + (2 if d == 0 else nx), 2), pl.ds(LEAD, ny)]
            dst = xrecv.at[par, d, p]
        elif d in Y_DIRS:
            src = ysend.at[d - 2, p]
            dst = yrecv.at[par, d - 2, p]
        else:
            src = ksend.at[d - 4, p]
            dst = krecv.at[par, d - 4, p]
        return pltpu.make_async_remote_copy(
            src_ref=src,
            dst_ref=dst,
            send_sem=send_sem.at[d, p],
            recv_sem=recv_sem.at[par, d, p],
            device_id=where[d],
            device_id_type=MESH,
        )

    def copy_coupling(d):
        if d in X_DIRS:
            src = c.at[:, 1 if d == 0 else nx]
            dst = c.at[:, nx + 1 if d == 0 else 0]
        else:
            src, dst = cysend.at[d - 2], cyrecv.at[d - 2]
        return pltpu.make_async_remote_copy(
            src_ref=src,
            dst_ref=dst,
            send_sem=csend_sem.at[d],
            recv_sem=crecv_sem.at[d],
            device_id=where[d],
            device_id_type=MESH,
        )

    def along_x(p, x, y, count):
        return pl.ds((p * planes + x + 2) * rows + LEAD + y, count, stride=rows)

    def start(dirs, par, p):
        for d in dirs:

            @pl.when(to[d])
            def _(d=d):
                copy(d, par, p).start()

    def send_y(par, p):
        for side, edge in enumerate(((0, 1), (ny - 1, ny - 2))):
            for n, y in enumerate(edge):
                ysend[side, p, n] = fa[along_x(p, 0, y, nx), :]
            start((2 + side,), par, p)
        for d in CORNERS:
            sx, sy = DIRECTIONS[d]
            x, y = (0 if sx < 0 else nx - 1), (0 if sy < 0 else ny - 1)
            ksend[d - 4, p] = va[p * planes + x + 2, pl.ds(LEAD + y, 1)]
        start(CORNERS, par, p)

    def receive(dirs, par, p):
        for d in dirs:

            @pl.when(from_[d])
            def _(d=d):
                sx, sy = DIRECTIONS[d]
                x, y = (nx if sx < 0 else -1), (ny if sy < 0 else -1)
                copy(d, par, p).wait_recv()
                if d in X_DIRS:
                    for n in range(2):
                        q = p * planes + (nx + 2 if d == 0 else 0) + n
                        va[q, pl.ds(LEAD, ny)] = xrecv[par, d, p, n]
                elif d in Y_DIRS:
                    fa[along_x(p, 0, y, nx), :] = yrecv[par, d - 2, p, 0]
                else:
                    va[p * planes + x + 2, pl.ds(LEAD + y, 1)] = krecv[par, d - 4, p]

    def wait_sent(p):
        for d in range(8):

            @pl.when(to[d])
            def _(d=d):
                copy(d, 0, p).wait_send()

    def first_send(p):
        load(p).wait()
        send_y(0, p)
        start(X_DIRS, 0, p)

    first_send(0)
    all_coupling().wait()
    lane = lax.broadcasted_iota(jnp.int32, (8, 128), 1)

    def clip_edges(i, _):
        for t in range(ny // 8):
            at = pl.ds(8 * t, 8)
            c[5, i, at] = jnp.where(lane == 127, 0.0, c[5, i, at])
            c[6, i, at] = jnp.where(lane == 0, 0.0, c[6, i, at])
        return 0

    lax.fori_loop(1, nx + 1, clip_edges, 0)
    for side, y in enumerate((0, ny - 1)):
        for k in range(7):
            cysend[side, k] = fc[pl.ds((k * (nx + 2) + 1) * ny + y, nx, stride=ny), :]
    for d in (2, 3, 0, 1):

        @pl.when(to[d])
        def _(d=d):
            copy_coupling(d).start()

    for p in range(1, np_):
        first_send(p)
    choose_sensors(nx, ny, nty, ntx, tx, ty, cell, frac, noise, slot, crowded, data, chosen, hot, weight, energy)
    for d in (0, 1, 2, 3):

        @pl.when(from_[d])
        def _(d=d):
            copy_coupling(d).wait_recv()

    def combine(coef, v, ahead, behind, up, down):
        r = coef[0] * v
        r = r + (coef[1] * ahead + coef[2] * behind)
        r = r + (coef[3] * up + coef[4] * down)
        return r + (coef[5] * pltpu.roll(v, 127, 1) + coef[6] * pltpu.roll(v, 1, 1))

    def sweep(src, dst, p, first, count, tiles):
        def at(x, t, off=0):
            return src[p * planes + x + 2, pl.ds(LEAD + 8 * t + off, 8)]

        def one(x, prev, cur):
            nxt = []
            for n, t in enumerate(tiles):
                coef = [c[k, x + 1, pl.ds(8 * t, 8)] for k in range(7)]
                ahead = at(x + 1, t)
                dst[p * planes + x + 2, pl.ds(LEAD + 8 * t, 8)] = combine(
                    coef, cur[n], ahead, prev[n], at(x, t, 1), at(x, t, -1)
                )
                nxt.append(ahead)
            return cur, tuple(nxt)

        carry = tuple(at(first - 1, t) for t in tiles), tuple(at(first, t) for t in tiles)
        for x in range(first, first + count):
            carry = one(x, *carry)

    def outer_rows(par, p):
        for side, y in enumerate((ny, -1)):
            inner = along = None
            for t in range(nx // 8):
                coef = [cyrecv[side, k, pl.ds(8 * t, 8)] for k in range(7)]
                v = fa[along_x(p, 8 * t, y, 8), :]
                ahead = fa[along_x(p, 8 * t + 1, y, 8), :]
                behind = fa[along_x(p, 8 * t - 1, y, 8), :]
                inner = fa[along_x(p, 8 * t, ny - 1 if side == 0 else 0, 8), :]
                outer = yrecv[par, side, p, 1, pl.ds(8 * t, 8)]
                up, down = (outer, inner) if side == 0 else (inner, outer)
                fb[along_x(p, 8 * t, y, 8), :] = combine(coef, v, ahead, behind, up, down)

    def work(block, _):
        for p in range(np_):
            work_on(block, p)
        return 0

    def work_on(block, p):
        par = lax.rem(block, 2)
        wait_sent(p)
        receive((0, 1, 4, 5, 6, 7, 2, 3), par, p)
        sweep(va, vb, p, -1, nx + 2, (0, 1, 2, 3))
        outer_rows(par, p)
        sweep(vb, va, p, 0, nx, (0, 3))

        @pl.when(block < blocks - 1)
        def _():
            send_y(1 - par, p)

        sweep(vb, va, p, 0, nx, (1, 2))

        @pl.when(block < blocks - 1)
        def _():
            start(X_DIRS, 1 - par, p)

        @pl.when(block == blocks - 1)
        def _():
            add_energy(nx, ny, p * planes + 2, va, hot, weight, energy)

    lax.fori_loop(0, blocks, work, 0)

    sensor_terms(chosen, energy, terms)
    offsets = [(k, a, b) for k in range(n_probe) for a in range(ntx) for b in range(nty)]
    place = {o: i for i, o in enumerate(offsets)}

    def far(o):
        k, a, b = o
        return min(k, n_probe - k) + min(a, ntx - a) / 2 + min(b, nty - b)

    for o in sorted(offsets[1:], key=far, reverse=True):
        k, a, b = o
        to_probe, to_tx, to_ty = lax.rem(me + k, n_probe), lax.rem(tx + a, ntx), lax.rem(ty + b, nty)
        pltpu.make_async_remote_copy(
            src_ref=terms.at[to_probe * ntx + to_tx],
            dst_ref=gathered.at[place[o]],
            send_sem=sum_send,
            recv_sem=sum_recv,
            device_id={"probe": to_probe, "tx": to_tx, "ty": to_ty},
            device_id_type=MESH,
        ).start()
    gathered[0] = terms[me * ntx + tx]
    for d in (0, 1, 2, 3):

        @pl.when(to[d])
        def _(d=d):
            copy_coupling(d).wait_send()

    others = gathered.at[pl.ds(1, len(offsets) - 1)]
    every = pltpu.make_async_remote_copy(
        src_ref=others,
        dst_ref=others,
        send_sem=sum_send,
        recv_sem=sum_recv,
        device_id={"probe": lax.rem(me + 1, n_probe)},
        device_id_type=MESH,
    )
    every.wait_recv()
    sums = [gathered[i] for i in range(8)]
    for i in range(8, len(offsets)):
        sums[i % 8] = sums[i % 8] + gathered[i]
    while len(sums) > 1:
        sums = [u + v for u, v in zip(sums[::2], sums[1::2])]
    lanes = cell.shape[1]
    width = lanes // nty
    result = sums[0]
    for b in range(1, nty):
        result = jnp.where(ty == b, pltpu.roll(sums[0], lanes - width * b, 1), result)
    out[...] = result[:, :width]
    every.wait_send()


def dot(a, b, dims=((1,), (0,)), **kw):
    return lax.dot_general(a, b, (dims, ((), ())), preferred_element_type=jnp.float32, **kw)


def split(x, count):
    pieces = []
    for _ in range(count):
        pieces.append(x.astype(jnp.bfloat16))
        x = x - pieces[-1].astype(jnp.float32)
    return pieces


def iota(shape, dim):
    return lax.broadcasted_iota(jnp.int32, shape, dim)


def choose_sensors(nx, ny, nty, ntx, tx, ty, cell, frac, noise, slot, crowded, data, chosen, hot, weight, energy):
    lines, lanes = cell.shape
    bf16, f32 = jnp.bfloat16, jnp.float32
    total_y = ny * nty
    shift_z = lanes.bit_length() - 1
    shift_x = shift_z + total_y.bit_length() - 1
    place = cell[...]
    global_x = lax.shift_right_logical(place, shift_x)
    global_y = lax.shift_right_logical(place, shift_z) & (total_y - 1)
    region = lax.div(global_x, nx) * nty + lax.div(global_y, ny)
    for r in range(ntx * nty):
        data[r : r + 1, :] = jnp.sum(jnp.where(region == r, 1.0, 0.0), axis=0, keepdims=True)
    most = jnp.max(jnp.sum(data[: ntx * nty, :], axis=1, keepdims=True))
    crowded[0, 0] = (most > CAPACITY).astype(jnp.int32)

    local_x, local_y = global_x - tx * nx, global_y - ty * ny
    inside = region == tx * nty + ty
    marks = jnp.where(inside, 1.0, 0.0).astype(bf16)
    upto = jnp.where(iota((lanes, lanes), 0) <= iota((lanes, lanes), 1), 1.0, 0.0).astype(bf16)
    before = jnp.where(iota((lines, lines), 1) < iota((lines, lines), 0), 1.0, 0.0).astype(bf16)
    within = dot(marks, upto)
    totals = dot(marks, jnp.ones((lanes, lanes), bf16))
    rank = dot(before, totals.astype(bf16)) + within - 1.0
    rank = jnp.where(inside, rank, -1.0).astype(jnp.int32)

    def as_float(x):
        return jnp.where(inside, x, 0).astype(f32)

    parts = [as_float(local_x), as_float(local_y), as_float(place & (lanes - 1)), jnp.where(inside, 1.0, 0.0)]
    parts += [lax.shift_right_logical(slot[...], shift_z).astype(f32), (slot[...] & (lanes - 1)).astype(f32)]
    parts += [x.astype(f32) for x in split(frac[...], 3) + split(noise[...], 3)]
    for k in range(16):
        data[pl.ds(k, lines, stride=16), :] = parts[k] if k < len(parts) else jnp.zeros((lines, lanes), f32)
    row_id = iota((CAPACITY, lanes), 0)
    picked = jnp.zeros((CAPACITY, 16), f32)
    for r in range(lines):
        one = jnp.where(rank[r : r + 1, :] == row_id, 1.0, 0.0).astype(bf16)
        picked = picked + dot(one, data[pl.ds(16 * r, 16), :].astype(bf16), ((1,), (1,)))
    chosen[...] = picked
    line = (picked[:, 0:1] * ny + picked[:, 1:2]).astype(jnp.int32)
    lane_id = iota((CAPACITY, lanes), 1)
    for b in range(nx * ny // lanes):
        hot[:, b * lanes : (b + 1) * lanes] = jnp.where(line - b * lanes == lane_id, 1.0, 0.0).astype(bf16)
    height = picked[:, 2:3].astype(jnp.int32)
    above = picked[:, 6:7] + picked[:, 7:8] + picked[:, 8:9]
    weight[...] = jnp.where(lane_id == height, 1.0 - above, 0.0) + jnp.where(lane_id == height + 1, above, 0.0)
    energy[...] = jnp.zeros_like(energy)


def add_energy(nx, ny, first, field, hot, weight, energy):
    lanes = field.shape[2]
    deep = 2 * lanes
    count = deep // ny
    got = jnp.zeros((CAPACITY, lanes), jnp.float32)
    for b in range(nx * ny // deep):
        cells = field[pl.ds(first + b * count, count), pl.ds(LEAD, ny)].reshape(deep, lanes)
        for piece in split(cells, 2):
            got = got + dot(hot[:, b * deep : (b + 1) * deep], piece)
    value = jnp.sum(got * weight[...], axis=1, keepdims=True)
    energy[...] += value * value


def sensor_terms(chosen, energy, terms):
    lines, _, lanes = terms.shape
    picked = chosen[...]
    valid, line, lane = (picked[:, k : k + 1].astype(jnp.int32) for k in (3, 4, 5))
    variance = picked[:, 9:10] + picked[:, 10:11] + picked[:, 11:12]
    grad = jnp.where(valid > 0, -energy[...] / jnp.where(valid > 0, variance, 1.0), 0.0)
    to_line = jnp.where(iota((CAPACITY, lines), 1) == line, 1.0, 0.0)
    to_lane = jnp.where(iota((CAPACITY, lanes), 1) == lane, grad, 0.0)
    ordered = dot(to_line, to_lane, ((0,), (0,)), precision=lax.Precision.HIGHEST)
    for n in range(lines):
        terms[n] = ordered[n : n + 1, :]


def whole(probes, coupling, cell, frac, noise, slot):
    np_, nx, ny, nz = probes.shape
    f32 = jnp.float32
    lines, lanes = cell.shape
    n, ntx, nty = lax.axis_size("probe"), lax.axis_size("tx"), lax.axis_size("ty")
    field = pltpu.VMEM((np_ * (nx + 4), ny + 2 * LEAD, nz), f32)
    vmem = pl.BlockSpec(memory_space=pltpu.VMEM)
    hbm = pl.BlockSpec(memory_space=pltpu.HBM)
    return pl.pallas_call(
        functools.partial(kernel, np_, nx, ny),
        out_shape=(
            jax.ShapeDtypeStruct((1, lanes // nty), f32),
            jax.ShapeDtypeStruct((1, 1), jnp.int32),
        ),
        in_specs=[hbm, hbm, vmem, vmem, vmem, vmem],
        out_specs=(vmem, pl.BlockSpec(memory_space=pltpu.SMEM)),
        scratch_shapes=[
            field,
            field,
            pltpu.VMEM((7, nx + 2, ny, nz), f32),
            pltpu.VMEM((2, 7, nx, nz), f32),
            pltpu.VMEM((2, 7, nx, nz), f32),
            pltpu.VMEM((2, 2, np_, 2, ny, nz), f32),
            pltpu.VMEM((2, 2, np_, 2, nx, nz), f32),
            pltpu.VMEM((2, 4, np_, 1, nz), f32),
            pltpu.VMEM((2, np_, 2, nx, nz), f32),
            pltpu.VMEM((4, np_, 1, nz), f32),
            pltpu.VMEM((16 * lines, lanes), f32),
            pltpu.VMEM((CAPACITY, 16), f32),
            pltpu.VMEM((CAPACITY, nx * ny), jnp.bfloat16),
            pltpu.VMEM((CAPACITY, lanes), f32),
            pltpu.VMEM((CAPACITY, 1), f32),
            pltpu.VMEM((lines, 1, lanes), f32),
            pltpu.VMEM((n * ntx * nty, 1, lanes), f32),
            pltpu.SemaphoreType.DMA((np_,)),
            pltpu.SemaphoreType.DMA,
            pltpu.SemaphoreType.DMA((8, np_)),
            pltpu.SemaphoreType.DMA((2, 8, np_)),
            pltpu.SemaphoreType.DMA((4,)),
            pltpu.SemaphoreType.DMA((4,)),
            pltpu.SemaphoreType.DMA,
            pltpu.SemaphoreType.DMA,
        ],
        compiler_params=pltpu.CompilerParams(collective_id=0, has_side_effects=True, vmem_limit_bytes=67_000_000),
        name="stencil",
    )(probes, coupling, cell, frac, noise, slot)


def general(probes, coupling, cell, frac, noise, slot):
    np_, nx, ny, nz = probes.shape

    def neighbour(block, axis, dim, step):
        count = lax.axis_size(axis)
        size = block.shape[dim]
        edge = lax.slice_in_dim(block, 0, 1, axis=dim) if step > 0 else lax.slice_in_dim(block, size - 1, size, axis=dim)
        edge = lax.ppermute(edge, axis, [(i, i - step) for i in range(count) if 0 <= i - step < count])
        if step > 0:
            return jnp.concatenate([lax.slice_in_dim(block, 1, None, axis=dim), edge], axis=dim)
        return jnp.concatenate([edge, lax.slice_in_dim(block, 0, size - 1, axis=dim)], axis=dim)

    def advance(_, v):
        deep = jnp.pad(v, ((0, 0), (0, 0), (0, 0), (1, 1)))
        r = coupling[0] * v
        r = r + coupling[1] * neighbour(v, "tx", 1, 1) + coupling[2] * neighbour(v, "tx", 1, -1)
        r = r + coupling[3] * neighbour(v, "ty", 2, 1) + coupling[4] * neighbour(v, "ty", 2, -1)
        return r + coupling[5] * deep[..., 2:] + coupling[6] * deep[..., :-2]

    field = lax.fori_loop(1, STEPS, advance, advance(0, probes)).reshape(np_, nx * ny, nz)
    total_y = ny * lax.axis_size("ty")
    local_x = cell // (total_y * nz) - lax.axis_index("tx") * nx
    local_y = cell // nz % total_y - lax.axis_index("ty") * ny
    height = (cell % nz)[:, None]
    inside = (local_x >= 0) & (local_x < nx) & (local_y >= 0) & (local_y < ny)
    line = jnp.clip(local_x, 0, nx - 1) * ny + jnp.clip(local_y, 0, ny - 1)
    heights = jnp.arange(nz, dtype=jnp.int32)[None, :]

    def energy(p, total):
        picked = jnp.take(field[p], line, axis=0)
        below = jnp.sum(jnp.where(heights == height, picked, 0.0), axis=1)
        above = jnp.sum(jnp.where(heights == height + 1, picked, 0.0), axis=1)
        value = (1.0 - frac) * below + frac * above
        return total + value * value

    energies = lax.fori_loop(0, np_, energy, jnp.zeros_like(frac))
    terms = jnp.where(inside, -energies / noise, 0.0)
    ordered = jnp.zeros_like(terms).at[slot].set(terms)
    return lax.psum_scatter(ordered, ("probe", "tx", "ty"), scatter_dimension=0, tiled=True)


def shards(probes, coupling, sensor_cell, sensor_frac, noise_var, owner_slot):
    numbers = (sensor_cell, sensor_frac, noise_var, owner_slot)
    gradient, crowded = whole(probes, coupling, *(a.reshape(-1, 128) for a in numbers))
    return lax.cond(crowded[0, 0] > 0, lambda: general(probes, coupling, *numbers), lambda: gradient.reshape(-1))


def solution(mesh):
    in_specs = (P("probe", "tx", "ty", None), P(None, "tx", "ty", None), P(), P(), P(), P())
    out_specs = P(("probe", "tx", "ty"))
    return jax.shard_map(shards, mesh=mesh, in_specs=in_specs, out_specs=out_specs, check_vma=False)
```
